1024 devices in a mesh: curve: 128 (over x, z), group: 8 (over y, core).
Axes of the slice: x: 4, y: 4, z: 32, core: 2. Of those that a mesh axis runs over, the one named last changes fastest.
Arguments:
- right_side: float32 [64, 262144], P(None, ('curve', 'group')), may hold values from -6 to 6
- start_field: float32 [64, 262144], P(None, ('curve', 'group')), may hold values from -3 to 3
- block_level: int32 [262144], P(('curve', 'group')), may hold values from 0 to 3
- neighbors: int32 [8, 262144], P(None, ('curve', 'group')), may hold values from -64 to 64, as said below
- neighbor_kinds: int32 [8, 262144], P(None, ('curve', 'group')), may hold values from 0 to 29
- owners_zero: int32 [2, 262144], P(None, ('curve', 'group')), may hold values from 0 to 63, as said below
- owners_one: int32 [2, 65536], P(None, 'curve'), may hold values from 0 to 127, as said below
- owners_two: int32 [2, 16384], P(None, 'curve'), may hold values from 0 to 31, as said below
- owners_three: int32 [2, 4096], replicated, may hold values from 0 to 7, as said below
- coarse_neighbors: int32 [8, 1024], replicated, may hold values from -1 to 1023, as said below
- coarse_kinds: int32 [8, 1024], replicated, may hold values from 0 to 29
- coarse_level: int32 [1024], replicated, may hold values from 0 to 3
- stiffness: float32 [64, 64], replicated
- smoother: float32 [64, 64], replicated
- couplings: float32 [30, 64, 64], replicated, may hold values from -0.18 to 0.18
- restriction: float32 [8, 64, 64], replicated, may hold values from -0.375 to 0.375
Outputs:
- smoothed: float32 [64, 262144], P(None, ('curve', 'group'))
The draws below stay inside these ranges and needn't reach their ends.
Inputs may be any that keep to these rules, and one draw needn't show every extreme that they name: `neighbors`: 0 where a slot couples to nothing, else the nonzero offset to another fine block inside the grid; in slot 0 the first block of each device's range has offset exactly -64 and the last exactly 64 wherever that neighbour exists. `owners_zero`: row 0: within each device's 256 blocks, slots of 64 level-one blocks that never fall, every slot used by 1 to 8 blocks and by 8 in some; row 1: octant. `owners_one`: row 0: within each curve index's level-one blocks, slots of 128 level-two blocks that never fall, every slot used by 1 to 8 blocks and by 8 in some; row 1: octant. `owners_two`: row 0: within each curve index's 128 blocks, slots of 32 level-three blocks that never fall, every slot used by 1 to 8 blocks and by 8 in some; row 1: octant. `owners_three`: row 0: within each curve index's 32 blocks, slots of 8 level-four blocks that never fall, every slot used by 1 to 8 blocks and by 8 in some; row 1: octant. `coarse_neighbors`: -1 where a slot couples to nothing, else another level-four block.
All inputs are finite; a program needn't handle non-finite values.
Results may differ from the reference program's by a relative error of at most 0.0003.
Values sent between devices are 32-bit elements; how exact they have to be, the bound alone decides.
No kernel may reach another device: no remote copies, remote signals or barrier semaphores. Data moves between devices by JAX's collectives and lax.ppermute only.
A program may use at most 64 MiB of HBM per device.

```python
import jax
import jax.numpy as jnp
from jax import lax

VALUES = 64
BLOCK_DEV = 256
FACE_SLOTS = 8
MORTAR_KINDS = 30
OCTANTS = 8
HALO_SPAN = 64
PRE_SWEEPS = 2
COARSE_SWEEPS = 3
LEVEL_ONE = 64
LEVEL_TWO = 128
LEVEL_THREE = 32
LEVEL_FOUR = 8
FINE_BLOCKS = 262144
BLOCKS_ONE = 65536
BLOCKS_TWO = 16384
BLOCKS_THREE = 4096
BLOCKS_FOUR = 1024
N_CURVE = 128
N_GROUP = 8


def family_lists(key, row_count, row_length):
    parent_count = row_length // 4
    key_pair, key_first, key_second, key_octant = jax.random.split(key, 4)
    paired = jax.random.randint(key_pair, (row_count, parent_count // 2), 1, 8)
    sizes = jnp.stack([paired, 8 - paired], axis=-1).reshape(row_count, parent_count)
    first_size = jax.random.randint(key_first, (row_count,), 1, 7)
    second_size = 1 + jax.random.randint(key_second, (row_count,), 0, 7 - first_size)
    third_size = 8 - first_size - second_size
    head_sizes = jnp.stack([jnp.full((row_count,), 8, jnp.int32), first_size, second_size, third_size], axis=-1)
    sizes = jnp.concatenate([head_sizes.astype(jnp.int32), sizes[:, 4:].astype(jnp.int32)], axis=1)
    ends = jnp.cumsum(sizes, axis=1)
    positions = jnp.arange(row_length, dtype=jnp.int32)
    parent = jnp.sum((ends[:, :, None] <= positions[None, None, :]).astype(jnp.int32), axis=1)
    octant = jax.random.randint(key_octant, (row_count, row_length), 0, 8)
    return jnp.stack([parent.reshape(-1), octant.reshape(-1)]).astype(jnp.int32)


def draw_owners_zero(key, part):
    return family_lists(jax.random.fold_in(key, 11), FINE_BLOCKS // BLOCK_DEV, BLOCK_DEV)


def draw_owners_one(key, part):
    return family_lists(jax.random.fold_in(key, 12), BLOCKS_ONE // (4 * LEVEL_TWO), 4 * LEVEL_TWO)


def draw_owners_two(key, part):
    return family_lists(jax.random.fold_in(key, 13), BLOCKS_TWO // LEVEL_TWO, LEVEL_TWO)


def draw_owners_three(key, part):
    return family_lists(jax.random.fold_in(key, 14), BLOCKS_THREE // LEVEL_THREE, LEVEL_THREE)


def draw_neighbors(key, part):
    key_step, key_sign, key_keep = jax.random.split(jax.random.fold_in(key, 21), 3)
    blocks = jnp.arange(FINE_BLOCKS, dtype=jnp.int32)[None, :]
    step_size = jax.random.randint(key_step, (FACE_SLOTS, FINE_BLOCKS), 1, HALO_SPAN + 1)
    direction = 2 * jax.random.randint(key_sign, (FACE_SLOTS, FINE_BLOCKS), 0, 2) - 1
    offset = direction * step_size
    keep_slot = jax.random.randint(key_keep, (FACE_SLOTS, FINE_BLOCKS), 0, 4) > 0
    slot_ids = jnp.arange(FACE_SLOTS, dtype=jnp.int32)[:, None]
    within = blocks % BLOCK_DEV
    force_back = (slot_ids == 0) & (within == 0)
    force_ahead = (slot_ids == 0) & (within == BLOCK_DEV - 1)
    offset = jnp.where(force_back, -HALO_SPAN, jnp.where(force_ahead, HALO_SPAN, offset))
    keep_slot = keep_slot | force_back | force_ahead
    target = blocks + offset
    inside = (target >= 0) & (target < FINE_BLOCKS)
    return jnp.where(keep_slot & inside, offset, 0).astype(jnp.int32)


def draw_coarse_neighbors(key, part):
    key_target, key_keep = jax.random.split(jax.random.fold_in(key, 31), 2)
    blocks = jnp.arange(BLOCKS_FOUR, dtype=jnp.int32)[None, :]
    target = jax.random.randint(key_target, (FACE_SLOTS, BLOCKS_FOUR), 0, BLOCKS_FOUR - 1)
    target = jnp.where(target >= blocks, target + 1, target)
    keep_slot = jax.random.randint(key_keep, (FACE_SLOTS, BLOCKS_FOUR), 0, 4) > 0
    return jnp.where(keep_slot, target, -1).astype(jnp.int32)


def draw_stiffness(key, part):
    inner_key = jax.random.fold_in(key, 41)
    spread = 0.05 * jax.random.normal(inner_key, (VALUES, VALUES), jnp.float32)
    return 2.0 * jnp.eye(VALUES, dtype=jnp.float32) + spread


def draw_smoother(key, part):
    inner_key = jax.random.fold_in(key, 42)
    spread = 0.0125 * jax.random.normal(inner_key, (VALUES, VALUES), jnp.float32)
    return 0.5 * jnp.eye(VALUES, dtype=jnp.float32) + spread


def set_ends(drawn, key, smallest, top_value):
    longest = drawn.shape.index(max(drawn.shape))
    spots = []
    for shift in (0, 1):
        where = [jax.random.randint(jax.random.fold_in(key, axis), (), 0, length) for axis, length in enumerate(drawn.shape)]
        where[longest] = (where[longest] + shift) % drawn.shape[longest]
        spots.append(tuple(where))
    return drawn.at[spots[0]].set(smallest).at[spots[1]].set(top_value)


def block_levels(own_key, dims, cuts, least, largest):
    def one(axis_at, blocks):
        heights = jax.random.uniform(jax.random.fold_in(jax.random.fold_in(own_key, 6), axis_at), (blocks,), jnp.float32, least / len(cuts), largest / len(cuts))
        return jnp.repeat(jnp.exp(heights), dims[axis_at] // blocks).reshape((-1,) + (1,) * (len(dims) - axis_at - 1))

    factor_of = one(*cuts[0])
    for cut in cuts[1:]:
        factor_of = factor_of * one(*cut)
    return factor_of


def noise(stream_key, shape, scale, bound, cuts=(), held_as=jnp.bfloat16):
    array = scale * jax.random.normal(stream_key, shape, jnp.float32)
    if cuts:
        array = array * block_levels(stream_key, shape, cuts, -0.22, 0.18)
    return jnp.clip(array, -bound, bound).astype(held_as)


def setup_inputs(seed: int = 0) -> dict:
    streams_of = jax.random.split(jax.random.key(seed), 17)
    right_side = noise(streams_of[0], (VALUES, FINE_BLOCKS), 1.0, 6.0, ((1, 1024),), jnp.float32)
    start_field = noise(streams_of[1], (VALUES, FINE_BLOCKS), 0.5, 3.0, ((1, 1024),), jnp.float32)
    block_level = set_ends(jax.random.randint(streams_of[2], (FINE_BLOCKS,), 0, 4), jax.random.fold_in(streams_of[2], 1), 0, 3).astype(jnp.int32)
    neighbors = draw_neighbors(jax.random.fold_in(streams_of[16], 71), 0)
    neighbor_kinds = set_ends(jax.random.randint(streams_of[4], (FACE_SLOTS, FINE_BLOCKS), 0, MORTAR_KINDS), jax.random.fold_in(streams_of[4], 1), 0, MORTAR_KINDS - 1).astype(jnp.int32)
    owners_zero = draw_owners_zero(jax.random.fold_in(streams_of[16], 71), 0)
    owners_one = draw_owners_one(jax.random.fold_in(streams_of[16], 71), 0)
    owners_two = draw_owners_two(jax.random.fold_in(streams_of[16], 71), 0)
    owners_three = draw_owners_three(jax.random.fold_in(streams_of[16], 71), 0)
    coarse_neighbors = draw_coarse_neighbors(jax.random.fold_in(streams_of[16], 71), 0)
    coarse_kinds = set_ends(jax.random.randint(streams_of[10], (FACE_SLOTS, BLOCKS_FOUR), 0, MORTAR_KINDS), jax.random.fold_in(streams_of[10], 1), 0, MORTAR_KINDS - 1).astype(jnp.int32)
    coarse_level = set_ends(jax.random.randint(streams_of[11], (BLOCKS_FOUR,), 0, 4), jax.random.fold_in(streams_of[11], 1), 0, 3).astype(jnp.int32)
    stiffness = draw_stiffness(jax.random.fold_in(streams_of[16], 71), 0)
    smoother = draw_smoother(jax.random.fold_in(streams_of[16], 71), 0)
    couplings = noise(streams_of[14], (MORTAR_KINDS, VALUES, VALUES), 0.03, 0.18, (), jnp.float32)
    restriction = noise(streams_of[15], (OCTANTS, VALUES, VALUES), 256 ** -0.5, 0.375, (), jnp.float32)
    return {"right_side": right_side, "start_field": start_field, "block_level": block_level, "neighbors": neighbors, "neighbor_kinds": neighbor_kinds, "owners_zero": owners_zero, "owners_one": owners_one, "owners_two": owners_two, "owners_three": owners_three, "coarse_neighbors": coarse_neighbors, "coarse_kinds": coarse_kinds, "coarse_level": coarse_level, "stiffness": stiffness, "smoother": smoother, "couplings": couplings, "restriction": restriction}


DAMPING = 0.7
PRECISE = lax.Precision.HIGHEST


def couple_sum(values, neighbor_index, kinds, couplings):
    is_valid = neighbor_index >= 0
    safe_index = jnp.where(is_valid, neighbor_index, 0)
    picked = jnp.take(values, safe_index.reshape(-1), axis=1)
    picked = picked.reshape(values.shape[0], neighbor_index.shape[0], neighbor_index.shape[1])
    picked = picked * is_valid[None].astype(jnp.float32)
    kind_ids = lax.broadcasted_iota(jnp.int32, (couplings.shape[0], 1, 1), 0)
    onehot = (kinds[None] == kind_ids).astype(jnp.float32)
    grouped = jnp.einsum("tkm,pkm->tpm", onehot, picked, precision=PRECISE)
    return jnp.einsum("tqp,tpm->qm", couplings, grouped, precision=PRECISE)


def apply_block(window, own_values, neighbor_index, kinds, scales, stiffness, couplings):
    inner_sum = jnp.dot(stiffness, own_values, precision=PRECISE) + couple_sum(window, neighbor_index, kinds, couplings)
    return scales[None, :] * inner_sum


def smooth_step(iterate, applied, rhs_values, scales, smoother):
    return iterate + DAMPING * jnp.dot(smoother, (rhs_values - applied) / scales[None, :], precision=PRECISE)


def octant_masks(octant, matrices):
    octant_ids = lax.broadcasted_iota(jnp.int32, (matrices.shape[0], 1, 1), 0)
    return (octant[None, None, :] == octant_ids).astype(jnp.float32)


def restrict(values, owners, parent_count, matrices):
    oct_masks = octant_masks(owners[1], matrices)
    mapped = jnp.einsum("oqp,opn->qn", matrices, values[None] * oct_masks, precision=PRECISE)
    slot_ids = lax.broadcasted_iota(jnp.int32, (1, parent_count), 1)
    onehot = (owners[0][:, None] == slot_ids).astype(jnp.float32)
    return jnp.dot(mapped, onehot, precision=PRECISE)


def prolong(values, owners, matrices):
    oct_masks = octant_masks(owners[1], matrices)
    slot_ids = lax.broadcasted_iota(jnp.int32, (1, values.shape[1]), 1)
    onehot = (owners[0][:, None] == slot_ids).astype(jnp.float32)
    pulled = jnp.dot(values, onehot.T, precision=PRECISE)
    mapped = jnp.einsum("oqp,qn->opn", matrices, pulled, precision=PRECISE)
    return jnp.sum(mapped * oct_masks, axis=0)


def grouped_restrict(values, owners, groups, parent_count, matrices):
    group_width = values.shape[1] // groups

    def per_group(group_index):
        first_col = group_index * group_width
        columns = lax.dynamic_slice_in_dim(values, first_col, group_width, 1)
        own_owners = lax.dynamic_slice_in_dim(owners, first_col, group_width, 1)
        return restrict(columns, own_owners, parent_count, matrices)

    pieces = lax.map(per_group, jnp.arange(groups, dtype=jnp.int32))
    return jnp.transpose(pieces, (1, 0, 2)).reshape(values.shape[0], groups * parent_count)


def grouped_prolong(values, owners, groups, matrices):
    parent_width = values.shape[1] // groups
    child_width = owners.shape[1] // groups

    def per_group(group_index):
        columns = lax.dynamic_slice_in_dim(values, group_index * parent_width, parent_width, 1)
        own_owners = lax.dynamic_slice_in_dim(owners, group_index * child_width, child_width, 1)
        return prolong(columns, own_owners, matrices)

    pieces = lax.map(per_group, jnp.arange(groups, dtype=jnp.int32))
    return jnp.transpose(pieces, (1, 0, 2)).reshape(values.shape[0], groups * child_width)


def fine_image(iterate, neighbors, kinds, scales, stiffness, couplings):
    padded = jnp.pad(iterate, ((0, 0), (HALO_SPAN, HALO_SPAN)))
    local_ids = jnp.arange(BLOCK_DEV, dtype=jnp.int32)[None, :]

    def per_device(device_index):
        first_block = (device_index * BLOCK_DEV).astype(jnp.int32)
        window = lax.dynamic_slice_in_dim(padded, first_block, BLOCK_DEV + 2 * HALO_SPAN, 1)
        own_values = lax.dynamic_slice_in_dim(iterate, first_block, BLOCK_DEV, 1)
        own_offset = lax.dynamic_slice_in_dim(neighbors, first_block, BLOCK_DEV, 1)
        own_kinds = lax.dynamic_slice_in_dim(kinds, first_block, BLOCK_DEV, 1)
        own_scales = lax.dynamic_slice_in_dim(scales, first_block, BLOCK_DEV, 0)
        window_index = jnp.where(own_offset != 0, local_ids + own_offset + HALO_SPAN, -1).astype(jnp.int32)
        return apply_block(window, own_values, window_index, own_kinds, own_scales, stiffness, couplings)

    pieces = lax.map(per_device, jnp.arange(N_CURVE * N_GROUP, dtype=jnp.int32))
    return jnp.transpose(pieces, (1, 0, 2)).reshape(iterate.shape[0], FINE_BLOCKS)


def reference(right_side, start_field, block_level, neighbors, neighbor_kinds, owners_zero, owners_one, owners_two, owners_three, coarse_neighbors, coarse_kinds, coarse_level, stiffness, smoother, couplings, restriction):
    scales = jnp.exp2(-block_level.astype(jnp.float32))
    iterate = start_field
    for sweep_index in range(PRE_SWEEPS):
        applied = fine_image(iterate, neighbors, neighbor_kinds, scales, stiffness, couplings)
        iterate = smooth_step(iterate, applied, right_side, scales, smoother)
    residual = right_side - fine_image(iterate, neighbors, neighbor_kinds, scales, stiffness, couplings)
    level_one = grouped_restrict(residual, owners_zero, N_CURVE * N_GROUP, LEVEL_ONE, restriction)
    level_two = grouped_restrict(level_one, owners_one, N_CURVE, LEVEL_TWO, restriction)
    level_three = grouped_restrict(level_two, owners_two, N_CURVE, LEVEL_THREE, restriction)
    coarse_rhs = grouped_restrict(level_three, owners_three, N_CURVE, LEVEL_FOUR, restriction)
    coarse_scales = jnp.exp2(-coarse_level.astype(jnp.float32))
    zero_field = jnp.zeros_like(coarse_rhs)
    correction = smooth_step(zero_field, zero_field, coarse_rhs, coarse_scales, smoother)
    for sweep_index in range(COARSE_SWEEPS - 1):
        applied = apply_block(correction, correction, coarse_neighbors, coarse_kinds, coarse_scales, stiffness, couplings)
        correction = smooth_step(correction, applied, coarse_rhs, coarse_scales, smoother)
    back_three = grouped_prolong(correction, owners_three, N_CURVE, restriction)
    back_two = grouped_prolong(back_three, owners_two, N_CURVE, restriction)
    back_one = grouped_prolong(back_two, owners_one, N_CURVE, restriction)
    back_zero = grouped_prolong(back_one, owners_zero, N_CURVE * N_GROUP, restriction)
    iterate = iterate + back_zero
    applied = fine_image(iterate, neighbors, neighbor_kinds, scales, stiffness, couplings)
    return smooth_step(iterate, applied, right_side, scales, smoother)
```

```python
import jax
import jax.numpy as jnp
from jax import lax
from jax.experimental import pallas as pl
from jax.experimental.pallas import tpu as pltpu
from jax.sharding import PartitionSpec as P

HALO = 64
DAMPING = 0.7
F32 = jnp.float32
BF16 = jnp.bfloat16
VMEM_LIMIT = 40 * 1024 * 1024


def halves(x):
    high = x.astype(BF16)
    return high, (x - high.astype(F32)).astype(BF16)


def nn(a, b):
    return lax.dot_general(a, b, (((1,), (0,)), ((), ())), preferred_element_type=F32)


def nt(a, b):
    return lax.dot_general(a, b, (((1,), (1,)), ((), ())), preferred_element_type=F32)


def corners(product):
    half = product.shape[1] // 2
    top, low = product[:64], product[64:]
    return top[:, :half] + (top[:, half:] + low[:, :half]) + low[:, half:]


def wide_dot(matrix_pair, x):
    high, low = halves(x)
    return corners(nn(matrix_pair, jnp.concatenate([high, low], axis=1)))


def stacked(x):
    return jnp.concatenate(halves(x), axis=0)


def folded(x):
    half = x.shape[0] // 2
    return x[:half] + x[half:]


def onehot_rows(row_count, columns):
    rows = lax.broadcasted_iota(jnp.int32, (row_count, columns.shape[1]), 0)
    return jnp.where(rows == columns, 1.0, 0.0).astype(BF16)


def left_by(x, lanes):
    size = x.shape[1]
    return pltpu.roll(x, (size - lanes) % size, axis=1)


def couple(slot_values, kinds, own, coupling_pair):
    total = None
    for part in range(8):
        pieces = []
        for kind in range(4 * part, 4 * part + 4):
            if kind < 30:
                chosen = None
                for slot in range(8):
                    term = jnp.where(kinds[slot : slot + 1] == kind, slot_values[slot], 0.0)
                    chosen = term if chosen is None else chosen + term
            elif kind == 30:
                chosen = own
            else:
                chosen = jnp.zeros_like(own)
            pieces.append(jnp.concatenate(halves(chosen), axis=1))
        block = jnp.concatenate(pieces, axis=0)
        product = nn(coupling_pair[:, 256 * part : 256 * part + 256], block)
        total = product if total is None else total + product
    return corners(total)


def fine_tile(window, offsets, kinds, coupling_pair, slots):
    lanes = lax.broadcasted_iota(jnp.int32, offsets.shape, 1)
    targets = jnp.where(offsets != 0, lanes + offsets + HALO, -1)
    window_pair = stacked(window)
    for slot in range(0, 8, 2):
        columns = jnp.concatenate([targets[slot : slot + 1], targets[slot + 1 : slot + 2]], axis=1)
        picked = folded(nn(window_pair, onehot_rows(256, columns)))
        slots[slot] = picked[:, :128]
        slots[slot + 1] = picked[:, 128:]
    own = left_by(window, HALO)[:, :128]
    return couple(slots, kinds, own, coupling_pair), own


def by_octant(x, octant):
    return jnp.concatenate([jnp.where(octant == which, x, 0.0) for which in range(8)], axis=0)


def restrict(x, slot, octant, restriction_pair, parents):
    mapped = wide_dot(restriction_pair, by_octant(x, octant))
    return folded(nt(stacked(mapped), onehot_rows(parents, slot)))


def prolong(x, slot, octant, back_pair):
    pulled = folded(nn(stacked(x), onehot_rows(x.shape[1], slot)))
    return wide_dot(back_pair, by_octant(pulled, octant))


def power(levels):
    return jnp.left_shift(jnp.ones_like(levels), levels).astype(F32)


def inverse_power(levels):
    return jnp.where(levels == 0, 1.0, jnp.where(levels == 1, 0.5, jnp.where(levels == 2, 0.25, 0.125)))


def prepare_kernel(
    place,
    couplings,
    stiffness,
    smoother,
    restriction,
    owners_one,
    owners_two,
    owners_three,
    coarse_neighbors,
    coarse_kinds,
    coarse_level,
    coupling_pair,
    smoother_pair,
    restriction_pair,
    back_pair,
    table,
):
    def store(target, first, x):
        high, low = halves(x)
        target[0:64, first : first + x.shape[1]] = high
        target[64:128, first : first + x.shape[1]] = low

    for part in range(15):
        store(
            coupling_pair,
            128 * part,
            jnp.concatenate([couplings[2 * part], couplings[2 * part + 1]], axis=1),
        )
    store(
        coupling_pair,
        1920,
        jnp.concatenate([stiffness[...], jnp.zeros((64, 64), F32)], axis=1),
    )
    store(smoother_pair, 0, DAMPING * smoother[...])
    for part in range(4):
        first, second = restriction[2 * part], restriction[2 * part + 1]
        store(restriction_pair, 128 * part, jnp.concatenate([first, second], axis=1))
        upright = jnp.concatenate([first, second], axis=0)
        square = jnp.concatenate([upright, jnp.zeros((128, 64), F32)], axis=1)
        store(back_pair, 128 * part, jnp.transpose(square)[0:64])

    member, group = place[0], place[1]
    lanes = lax.broadcasted_iota(jnp.int32, (8, 128), 1)

    def own(ref, rows, block, per, valid):
        share = 128 // per
        first = pl.multiple_of((block // share) * 128, 128)
        held = ref[0:rows, pl.ds(first, 128)]
        if rows == 1:
            held = jnp.broadcast_to(held, (8, 128))
        shift = lax.rem(128 - per * lax.rem(block, share), 128)
        moved = pltpu.roll(held, shift, axis=1)
        return jnp.where(lanes < per, moved, valid)

    def rows_of(ref, block, per):
        share = 128 // per
        first = pl.multiple_of((block // share) * 128, 128)
        shift = lax.rem(128 - per * lax.rem(block, share), 128)
        made = []
        for row in range(2):
            held = jnp.broadcast_to(ref[row : row + 1, pl.ds(first, 128)], (8, 128))
            moved = held if per == 128 else pltpu.roll(held, shift, axis=1)
            made.append(jnp.where(lanes < per, moved, -1)[0:1])
        return made

    zero = jnp.int32(0)
    for at, (ref, block, per) in enumerate(
        ((owners_one, group, 64), (owners_two, zero, 128), (owners_three, member, 32))
    ):
        slot, octant = rows_of(ref, block, per)
        table[2 * at : 2 * at + 1] = slot
        table[2 * at + 1 : 2 * at + 2] = octant
    table[6:7] = own(coarse_level, 1, member, 8, 0)[0:1]
    table[7:8] = jnp.zeros((1, 128), jnp.int32)
    near = own(coarse_neighbors, 8, member, 8, -1)
    table[8:16] = near
    table[16:24] = jnp.where(near >= 0, own(coarse_kinds, 8, member, 8, -1), -1)


def pack_kernel(right_side, start_field, block_level, neighbors, neighbor_kinds, up, down):
    lane = lax.broadcasted_iota(jnp.int32, (32, 128), 1)
    low, high = start_field[:, 0:128], start_field[:, 128:256]
    up[0:64] = high
    up[64:96] = jnp.where(lane < 64, left_by(low[0:32], 64), low[32:64])
    down[0:64] = low
    down[64:96] = jnp.where(lane < 64, high[0:32], left_by(high[32:64], 64))
    for target, columns in ((up, slice(128, 256)), (down, slice(0, 128))):
        target[96:160] = right_side[:, columns]
        target[160:168] = neighbors[:, columns].astype(F32)
        target[168:176] = neighbor_kinds[:, columns].astype(F32)
        target[176:184] = jnp.broadcast_to(block_level[:, columns], (8, 128)).astype(F32)


def before_kernel(
    left,
    right_side,
    start_field,
    block_level,
    neighbors,
    neighbor_kinds,
    right,
    owners_zero,
    coupling_pair,
    smoother_pair,
    restriction_pair,
    table,
    iterate_out,
    part_out,
    first,
    second,
    third,
    facts_wide,
    facts_narrow,
    remainder,
    slots,
):
    matrix = coupling_pair
    far_left, far_right = left[64:96], right[64:96]
    row = jnp.concatenate(
        [
            jnp.concatenate([left_by(far_left, 64), far_left], axis=0),
            left[0:64],
            start_field[...],
            right[0:64],
            jnp.concatenate([far_right, left_by(far_right, 64)], axis=0),
        ],
        axis=1,
    )
    first[...] = left_by(row, 64)[:, :640]
    numbers = jnp.concatenate(
        [
            neighbors[...],
            neighbor_kinds[...],
            jnp.broadcast_to(block_level[...], (8, 256)),
        ],
        axis=0,
    )
    own = jnp.concatenate([right_side[...], numbers.astype(F32)], axis=0)
    facts = jnp.concatenate([left[96:184], own, right[96:184]], axis=1)
    facts_wide[...] = facts
    facts_narrow[...] = left_by(facts, 64)[:, :384]

    def image(source, facts_of, at):
        start = pl.multiple_of(128 * at, 128)
        window = source[:, pl.ds(start, 256)]
        here = facts_of[:, pl.ds(start, 128)]
        offsets = here[64:72].astype(jnp.int32)
        kinds = here[72:80].astype(jnp.int32)
        levels = here[80:81].astype(jnp.int32)
        applied, held = fine_tile(window, offsets, kinds, matrix[...], slots)
        return start, here[0:64], levels, applied, held

    def sweep(source, facts_of, target):
        def one(at, carry):
            start, rhs, levels, applied, held = image(source, facts_of, at)
            change = wide_dot(smoother_pair[...], rhs * power(levels) - applied)
            target[:, pl.ds(start, 128)] = held + change
            return carry

        return one

    lax.fori_loop(0, 4, sweep(first, facts_wide, second), 0)
    lax.fori_loop(0, 3, sweep(second, facts_narrow, third), 0)

    def last(at, carry):
        start, rhs, levels, applied, held = image(third, facts_wide.at[:, 128:384], at)
        remainder[:, pl.ds(start, 128)] = rhs - inverse_power(levels) * applied
        iterate_out[:, pl.ds(start, 128)] = held
        return carry

    lax.fori_loop(0, 2, last, 0)

    r_pair = restriction_pair[...]
    one = restrict(remainder[...], owners_zero[0:1], owners_zero[1:2], r_pair, 128)
    two = restrict(one, table[0:1], table[1:2], r_pair, 128)
    three = restrict(two, table[2:3], table[3:4], r_pair, 128)
    four = restrict(three, table[4:5], table[5:6], r_pair, 128)
    four = four * power(table[6:7])
    both = jnp.concatenate([four, left_by(four, 4)], axis=0)
    part_out[...] = jnp.transpose(both)[0:4]


def coarse_kernel(
    place,
    gathered,
    table,
    coarse_neighbors,
    coarse_kinds,
    coupling_pair,
    smoother_pair,
    back_pair,
    owners_zero,
    iterate,
    iterate_out,
    low_edge,
    high_edge,
    slots,
):
    member = place[0]
    field_pair = stacked(jnp.transpose(gathered[...]))
    s_pair = smoother_pair[...]
    matrix = coupling_pair[...]

    def gather(blocks):
        known = blocks >= 0
        rows = jnp.where(known, 4 * (blocks >> 3) + (blocks & 3), -1)
        both = folded(nn(field_pair, onehot_rows(512, rows)))
        return jnp.where(((blocks >> 2) & 1) == 0, both[0:64], both[64:128])

    lanes = lax.broadcasted_iota(jnp.int32, (1, 128), 1)
    near = table[8:16]
    near_kinds = table[16:24]
    wanted = jnp.where((lanes >= 64) & (lanes < 72), 8 * member + lanes - 64, -1)
    for slot in range(8):
        moved = pltpu.roll(near, 8 * slot, axis=1) if slot else near
        wanted = jnp.where((lanes >> 3) == slot, moved[slot : slot + 1], wanted)
    shifted = coarse_neighbors[...] + 1
    facts = jnp.concatenate(
        [shifted >> 5, shifted & 31, coarse_kinds[...], jnp.zeros_like(shifted)], axis=0
    ).astype(F32).astype(BF16)
    found = nn(facts, onehot_rows(1024, wanted)).astype(jnp.int32)
    links = 32 * found[0:8] + found[8:16] - 1
    link_kinds = found[16:24]

    for slot in range(0, 8, 2):
        blocks = jnp.concatenate([links[slot : slot + 1], links[slot + 1 : slot + 2]], axis=1)
        swept = wide_dot(s_pair, gather(blocks))
        slots[slot] = swept[:, :128]
        slots[slot + 1] = swept[:, 128:]
    rhs = gather(wanted)
    once = wide_dot(s_pair, rhs)
    twice = once + wide_dot(s_pair, rhs - couple(slots, link_kinds, once, matrix))
    for slot in range(8):
        slots[slot] = left_by(twice, 8 * slot) if slot else twice
    held = left_by(twice, 64)
    applied = couple(slots, near_kinds, held, matrix)
    correction = held + wide_dot(s_pair, left_by(rhs, 64) - applied)

    b_pair = back_pair[...]
    three = prolong(correction, table[4:5], table[5:6], b_pair)
    two = prolong(three, table[2:3], table[3:4], b_pair)
    one = prolong(two, table[0:1], table[1:2], b_pair)
    zero = prolong(one, owners_zero[0:1], owners_zero[1:2], b_pair)
    field = iterate[...] + zero
    iterate_out[...] = field
    low, high = field[:, 0:128], left_by(field[:, 128:256], 64)
    lane = lax.broadcasted_iota(jnp.int32, (32, 128), 1)
    low_edge[...] = jnp.where(lane < 64, low[0:32], left_by(low[32:64], 64))
    high_edge[...] = jnp.where(lane < 64, high[0:32], left_by(high[32:64], 64))


def after_kernel(
    left,
    field,
    right,
    right_side,
    block_level,
    neighbors,
    neighbor_kinds,
    coupling_pair,
    smoother_pair,
    out,
    window_all,
    slots,
):
    def wide(edge):
        return jnp.concatenate([edge[...], left_by(edge[...], 64)], axis=0)

    row = jnp.concatenate([wide(left), field[...], wide(right)], axis=1)
    lanes = lax.broadcasted_iota(jnp.int32, (64, 384), 1)
    body = left_by(row, 64)
    window_all[...] = jnp.where(lanes < 64, row[:, 0:384], body[:, 0:384])

    def one(at, carry):
        start = pl.multiple_of(128 * at, 128)
        columns = pl.ds(start, 128)
        applied, held = fine_tile(
            window_all[:, pl.ds(start, 256)],
            neighbors[:, columns],
            neighbor_kinds[:, columns],
            coupling_pair[...],
            slots,
        )
        rhs = right_side[:, columns] * power(block_level[:, columns])
        out[:, pl.ds(start, 128)] = held + wide_dot(
            smoother_pair[...], rhs - applied
        )
        return carry

    lax.fori_loop(0, 2, one, 0)


def call(kernel, outs, scratch, name, flops, *args, scalars=0):
    specs = [pl.BlockSpec(memory_space=pltpu.SMEM)] * scalars
    specs += [pl.BlockSpec(memory_space=pltpu.VMEM)] * (len(args) - scalars)
    return pl.pallas_call(
        kernel,
        out_shape=[jax.ShapeDtypeStruct(shape, dtype) for shape, dtype in outs],
        in_specs=specs,
        out_specs=[pl.BlockSpec(memory_space=pltpu.VMEM)] * len(outs),
        scratch_shapes=[pltpu.VMEM(shape, dtype) for shape, dtype in scratch],
        compiler_params=pltpu.CompilerParams(vmem_limit_bytes=VMEM_LIMIT),
        cost_estimate=pl.CostEstimate(flops=flops, bytes_accessed=1 << 20, transcendentals=0),
        name=name,
    )(*args)


AXES = ("curve", "group")


def both_ways(up_part, down_part):
    peers = lax.axis_size(AXES)
    up = [(i, i + 1) for i in range(peers - 1)]
    down = [(i + 1, i) for i in range(peers - 1)]
    return lax.ppermute(up_part, AXES, up), lax.ppermute(down_part, AXES, down)


DEPTH = 32
WIDTH = 4


def spread(x, axis, count, groups=None):
    copies = jnp.broadcast_to(x[None], (count,) + x.shape)
    return lax.all_to_all(copies, axis, 0, 0, axis_index_groups=groups)


def share_coarse(part):
    along_z = [[x * DEPTH + z for z in range(DEPTH)] for x in range(WIDTH)]
    along_x = [[x * DEPTH + z for x in range(WIDTH)] for z in range(DEPTH)]
    total = jnp.sum(spread(part, "group", 8), axis=0)
    column = spread(total, "curve", DEPTH, along_z)
    return spread(column, "curve", WIDTH, along_x)


def stage_prepare(place, *args):
    outs = (
        ((128, 2048), BF16),
        ((128, 64), BF16),
        ((128, 512), BF16),
        ((128, 512), BF16),
        ((24, 128), jnp.int32),
    )
    return call(prepare_kernel, outs, (), "prepare", 1 << 20, place, *args, scalars=1)


def stage_before(*args):
    outs = (((64, 256), F32), ((4, 128), F32))
    scratch = (
        ((64, 640), F32),
        ((64, 512), F32),
        ((64, 384), F32),
        ((88, 512), F32),
        ((88, 384), F32),
        ((64, 256), F32),
        ((8, 64, 128), F32),
    )
    return call(before_kernel, outs, scratch, "before", 1 << 31, *args)


def stage_coarse(place, *args):
    outs = (((64, 256), F32), ((32, 128), F32), ((32, 128), F32))
    scratch = (((8, 64, 128), F32),)
    return call(coarse_kernel, outs, scratch, "coarse", 1 << 30, place, *args, scalars=1)


def stage_after(*args):
    scratch = (((64, 384), F32), ((8, 64, 128), F32))
    return call(after_kernel, (((64, 256), F32),), scratch, "after", 1 << 29, *args)


def stage_pack(*args):
    outs = (((184, 128), F32), ((184, 128), F32))
    return call(pack_kernel, outs, (), "pack", 1 << 20, *args)


def shards(
    right_side,
    start_field,
    block_level,
    neighbors,
    neighbor_kinds,
    owners_zero,
    owners_one,
    owners_two,
    owners_three,
    coarse_neighbors,
    coarse_kinds,
    coarse_level,
    stiffness,
    smoother,
    couplings,
    restriction,
):
    place = jnp.stack([lax.axis_index("curve"), lax.axis_index("group")]).astype(jnp.int32)
    fine = (right_side, start_field, block_level[None, :], neighbors, neighbor_kinds)
    left, right = both_ways(*stage_pack(*fine))
    coupling_pair, smoother_pair, restriction_pair, back_pair, table = stage_prepare(
        place,
        couplings,
        stiffness,
        smoother,
        restriction,
        owners_one,
        owners_two,
        owners_three,
        coarse_neighbors,
        coarse_kinds,
        coarse_level[None, :],
    )
    iterate, part = stage_before(
        left, *fine, right, owners_zero, coupling_pair, smoother_pair, restriction_pair, table
    )
    gathered = share_coarse(part)
    gathered = gathered.reshape(-1, gathered.shape[-1])
    field, low_edge, high_edge = stage_coarse(
        place,
        gathered,
        table,
        coarse_neighbors,
        coarse_kinds,
        coupling_pair,
        smoother_pair,
        back_pair,
        owners_zero,
        iterate,
    )
    left_edge, right_edge = both_ways(high_edge, low_edge)
    (out,) = stage_after(
        left_edge,
        field,
        right_edge,
        right_side,
        block_level[None, :],
        neighbors,
        neighbor_kinds,
        coupling_pair,
        smoother_pair,
    )
    return out


def solution(mesh):
    fine = P(None, ("curve", "group"))
    return jax.shard_map(
        shards,
        mesh=mesh,
        in_specs=(
            fine,
            fine,
            P(("curve", "group")),
            fine,
            fine,
            fine,
            P(None, "curve"),
            P(None, "curve"),
            P(),
            P(),
            P(),
            P(),
            P(),
            P(),
            P(),
            P(),
        ),
        out_specs=fine,
        check_vma=False,
    )
```

```python
import jax
import jax.numpy as jnp
from jax import lax
from jax.experimental import pallas as pl
from jax.experimental.pallas import tpu as pltpu
from jax.sharding import PartitionSpec as P

HALO = 64
DAMPING = 0.7
F32 = jnp.float32
BF16 = jnp.bfloat16
VMEM_LIMIT = 40 * 1024 * 1024
PACK_LIMIT = 60 * 1024 * 1024


def halves(x):
    high = x.astype(BF16)
    return high, (x - high.astype(F32)).astype(BF16)


def nn(a, b):
    return lax.dot_general(a, b, (((1,), (0,)), ((), ())), preferred_element_type=F32)


def nt(a, b):
    return lax.dot_general(a, b, (((1,), (1,)), ((), ())), preferred_element_type=F32)


def corners(product):
    half = product.shape[1] // 2
    top, low = product[:64], product[64:]
    return top[:, :half] + (top[:, half:] + low[:, :half]) + low[:, half:]


def wide_dot(matrix_pair, x):
    high, low = halves(x)
    return corners(nn(matrix_pair, jnp.concatenate([high, low], axis=1)))


def stacked(x):
    return jnp.concatenate(halves(x), axis=0)


def folded(x):
    half = x.shape[0] // 2
    return x[:half] + x[half:]


def onehot_rows(row_count, columns):
    rows = lax.broadcasted_iota(jnp.int32, (row_count, columns.shape[1]), 0)
    return jnp.where(rows == columns, 1.0, 0.0).astype(BF16)


def left_by(x, lanes):
    size = x.shape[1]
    return pltpu.roll(x, (size - lanes) % size, axis=1)


def couple(values, kinds, own, coupling_pair):
    total = None
    for part in range(8):
        pieces = []
        for kind in range(4 * part, 4 * part + 4):
            if kind < 30:
                chosen = None
                for slot in range(8):
                    term = jnp.where(kinds[slot : slot + 1] == kind, values[slot], 0.0)
                    chosen = term if chosen is None else chosen + term
            elif kind == 30:
                chosen = own
            else:
                chosen = jnp.zeros_like(own)
            pieces.append(jnp.concatenate(halves(chosen), axis=1))
        block = jnp.concatenate(pieces, axis=0)
        product = nn(coupling_pair[:, 256 * part : 256 * part + 256], block)
        total = product if total is None else total + product
    return corners(total)


def fine_tile(window, offsets, kinds, coupling_pair):
    lanes = lax.broadcasted_iota(jnp.int32, offsets.shape, 1)
    targets = jnp.where(offsets != 0, lanes + offsets + HALO, -1)
    window_pair = stacked(window)
    values = []
    for slot in range(0, 8, 2):
        columns = jnp.concatenate([targets[slot : slot + 1], targets[slot + 1 : slot + 2]], axis=1)
        picked = folded(nn(window_pair, onehot_rows(256, columns)))
        values += [picked[:, :128], picked[:, 128:]]
    own = left_by(window, HALO)[:, :128]
    return couple(values, kinds, own, coupling_pair), own


def by_octant(x, octant):
    return jnp.concatenate([jnp.where(octant == which, x, 0.0) for which in range(8)], axis=0)


def restrict(x, slot, octant, restriction_pair, parents):
    mapped = wide_dot(restriction_pair, by_octant(x, octant))
    return folded(nt(stacked(mapped), onehot_rows(parents, slot)))


def prolong(x, slot, octant, back_pair):
    pulled = folded(nn(stacked(x), onehot_rows(x.shape[1], slot)))
    return wide_dot(back_pair, by_octant(pulled, octant))


def power(levels):
    return jnp.left_shift(jnp.ones_like(levels), levels).astype(F32)


def inverse_power(levels):
    return jnp.where(levels == 0, 1.0, jnp.where(levels == 1, 0.5, jnp.where(levels == 2, 0.25, 0.125)))


def own_lanes(ref, rows, block, per):
    share = 128 // per
    first = pl.multiple_of((block // share) * 128, 128)
    held = ref[rows, pl.ds(first, 128)]
    held = jnp.broadcast_to(held, (8, 128))
    if share > 1:
        held = pltpu.roll(held, lax.rem(128 - per * lax.rem(block, share), 128), axis=1)
    lanes = lax.broadcasted_iota(jnp.int32, (8, 128), 1)
    return jnp.where(lanes < per, held, -1)


def other_curve(member, group):
    return jnp.where(
        group == 0,
        jnp.maximum(member - 1, 0),
        jnp.where(group == 7, jnp.minimum(member + 1, 127), member),
    )


def prepare_kernel(
    place,
    couplings,
    stiffness,
    smoother,
    restriction,
    owners_one,
    owners_two,
    owners_three,
    coarse_neighbors,
    coarse_kinds,
    coarse_level,
    coupling_pair,
    smoother_pair,
    restriction_pair,
    back_pair,
    table,
):
    def store(target, first, x):
        high, low = halves(x)
        target[0:64, first : first + x.shape[1]] = high
        target[64:128, first : first + x.shape[1]] = low

    for part in range(15):
        store(
            coupling_pair,
            128 * part,
            jnp.concatenate([couplings[2 * part], couplings[2 * part + 1]], axis=1),
        )
    store(
        coupling_pair,
        1920,
        jnp.concatenate([stiffness[...], jnp.zeros((64, 64), F32)], axis=1),
    )
    store(smoother_pair, 0, DAMPING * smoother[...])
    for part in range(4):
        first, second = restriction[2 * part], restriction[2 * part + 1]
        store(restriction_pair, 128 * part, jnp.concatenate([first, second], axis=1))
        upright = jnp.concatenate([first, second], axis=0)
        square = jnp.concatenate([upright, jnp.zeros((128, 64), F32)], axis=1)
        store(back_pair, 128 * part, jnp.transpose(square)[0:64])

    member, group = place[0], place[1]
    other = other_curve(member, group)
    lanes = lax.broadcasted_iota(jnp.int32, (8, 128), 1)

    def row(at):
        return slice(at, at + 1)

    mine = own_lanes(owners_three, row(0), member, 32)
    theirs = own_lanes(owners_three, row(0), other, 32)
    theirs = jnp.where(theirs < 0, -1, theirs + 8)
    table[0:1] = jnp.concatenate([mine, theirs], axis=1)[0:1]
    table[1:2] = jnp.concatenate(
        [
            own_lanes(owners_three, row(1), member, 32),
            own_lanes(owners_three, row(1), other, 32),
        ],
        axis=1,
    )[0:1]
    level = jnp.maximum(own_lanes(coarse_level, row(0), member, 8), 0)
    zero = jnp.int32(0)
    for at, values in enumerate(
        (
            level,
            own_lanes(owners_one, row(0), group, 64),
            own_lanes(owners_one, row(1), group, 64),
            own_lanes(owners_two, row(0), zero, 128),
            own_lanes(owners_two, row(1), zero, 128),
            jnp.zeros_like(level),
        )
    ):
        table[2 + at : 3 + at] = jnp.concatenate([values, values], axis=1)[0:1]
    every = slice(0, 8)
    wanted, near_kinds = [], []
    for curve in (member, other):
        near = own_lanes(coarse_neighbors, every, curve, 8)
        near_kinds.append(jnp.where(near >= 0, own_lanes(coarse_kinds, every, curve, 8), -1))
        blocks = jnp.where((lanes >= 64) & (lanes < 72), 8 * curve + lanes - 64, -1)
        for slot in range(8):
            moved = pltpu.roll(near, 8 * slot, axis=1) if slot else near
            moved = jnp.broadcast_to(moved[slot : slot + 1], (8, 128))
            blocks = jnp.where((lanes >> 3) == slot, moved, blocks)
        wanted.append(blocks)
    wanted = jnp.concatenate(wanted, axis=1)[0:1]
    both_kinds = jnp.where(lanes < 8, near_kinds[0], pltpu.roll(near_kinds[1], 8, axis=1))
    shifted = coarse_neighbors[...] + 1
    facts = jnp.concatenate(
        [shifted >> 5, shifted & 31, coarse_kinds[...], jnp.zeros_like(shifted)], axis=0
    )
    facts = facts.astype(F32).astype(BF16)
    found = nn(facts, onehot_rows(1024, wanted)).astype(jnp.int32)
    table[8:16] = 32 * found[0:8] + found[8:16] - 1
    table[16:24] = found[16:24]
    table[24:32] = jnp.concatenate([both_kinds, both_kinds], axis=1)
    table[32:40] = jnp.broadcast_to(wanted, (8, 256))


def pack_kernel(
    place,
    right_side,
    start_field,
    block_level,
    neighbors,
    neighbor_kinds,
    owners_zero,
    owners_one,
    owners_two,
    up,
    down,
    field,
    facts,
    parents,
):
    lane = lax.broadcasted_iota(jnp.int32, (32, 128), 1)
    low, high = start_field[:, 0:128], start_field[:, 128:256]
    up[0:64] = high
    up[64:96] = jnp.where(lane < 64, left_by(low[0:32], 64), low[32:64])
    down[0:64] = low
    down[64:96] = jnp.where(lane < 64, high[0:32], left_by(high[32:64], 64))
    field[...] = start_field[...]
    facts[0:64] = right_side[...]
    facts[64:72] = neighbors[...].astype(F32)
    facts[72:80] = neighbor_kinds[...].astype(F32)
    facts[80:88] = jnp.broadcast_to(block_level[...], (8, 256)).astype(F32)
    parents[...] = jnp.concatenate([owners_zero[...]] * 4, axis=0)
    group = place[1]
    shared = [
        own_lanes(owners_one, slice(0, 1), group, 64),
        own_lanes(owners_one, slice(1, 2), group, 64),
        jnp.broadcast_to(owners_two[0:1, :], (8, 128)),
        jnp.broadcast_to(owners_two[1:2, :], (8, 128)),
    ]
    for target, columns in ((up, slice(128, 256)), (down, slice(0, 128))):
        target[96:184] = facts[:, columns]
        target[184:186] = owners_zero[:, columns].astype(F32)
        for at, values in enumerate(shared):
            target[186 + at : 187 + at] = values[0:1].astype(F32)
        target[190:192] = jnp.zeros((2, 128), F32)


def fine_step(window, here, coupling_pair):
    offsets = here[64:72].astype(jnp.int32)
    kinds = here[72:80].astype(jnp.int32)
    levels = here[80:81].astype(jnp.int32)
    applied, held = fine_tile(window, offsets, kinds, coupling_pair)
    return applied, held, here[0:64], levels


def before_kernel(
    left,
    start_field,
    facts,
    right,
    owners_zero,
    coupling_pair,
    smoother_pair,
    restriction_pair,
    table,
    iterate_out,
    part_out,
    first,
    second,
    facts_wide,
    facts_narrow,
    remainder,
):
    matrix = coupling_pair
    far_left, far_right = left[64:96], right[64:96]
    row = jnp.concatenate(
        [
            jnp.concatenate([left_by(far_left, 64), far_left], axis=0),
            left[0:64],
            start_field[...],
            right[0:64],
            jnp.concatenate([far_right, left_by(far_right, 64)], axis=0),
        ],
        axis=1,
    )
    first[...] = left_by(row, 64)[:, :640]
    wide = jnp.concatenate([left[96:184], facts[...], right[96:184]], axis=1)
    facts_wide[...] = wide
    facts_narrow[...] = left_by(wide, 64)[:, :384]

    def sweep(source, facts_of, target, tiles):
        for at in range(tiles):
            columns = slice(128 * at, 128 * at + 128)
            applied, held, rhs, levels = fine_step(
                source[:, 128 * at : 128 * at + 256], facts_of[:, columns], matrix[...]
            )
            change = wide_dot(smoother_pair[...], rhs * power(levels) - applied)
            target[:, columns] = held + change

    sweep(first, facts_wide, second, 4)
    sweep(second, facts_narrow, iterate_out, 3)
    for at in range(2):
        columns = slice(128 * at, 128 * at + 128)
        applied, held, rhs, levels = fine_step(
            iterate_out[:, 128 * at : 128 * at + 256], facts[:, columns], matrix[...]
        )
        remainder[:, columns] = rhs - inverse_power(levels) * applied

    r_pair = restriction_pair[...]
    one = restrict(remainder[...], owners_zero[0:1], owners_zero[1:2], r_pair, 128)
    two = restrict(one, table[3:4, :128], table[4:5, :128], r_pair, 128)
    three = restrict(two, table[5:6, :128], table[6:7, :128], r_pair, 128)
    four = restrict(three, table[0:1, :128], table[1:2, :128], r_pair, 128)
    four = four * power(table[2:3, :128])
    both = jnp.concatenate([four, left_by(four, 4)], axis=0)
    part_out[...] = jnp.transpose(both)[0:4]


def finish_kernel(
    place,
    gathered,
    table,
    left,
    right,
    owners_zero,
    coupling_pair,
    smoother_pair,
    back_pair,
    iterate,
    facts,
    out,
    window,
):
    group = place[1]
    field_pair = stacked(jnp.transpose(gathered[...]))
    s_pair = smoother_pair[...]
    matrix = coupling_pair[...]

    def gather(blocks):
        rows = jnp.where(blocks >= 0, 4 * (blocks >> 3) + (blocks & 3), -1)
        both = folded(nn(field_pair, onehot_rows(512, rows)))
        return jnp.where(((blocks >> 2) & 1) == 0, both[0:64], both[64:128])

    values = [wide_dot(s_pair, gather(table[8 + slot : 9 + slot])) for slot in range(8)]
    rhs = gather(table[32:33])
    once = wide_dot(s_pair, rhs)
    twice = []
    for half in (slice(0, 128), slice(128, 256)):
        applied = couple([v[:, half] for v in values], table[16:24, half], once[:, half], matrix)
        twice.append(once[:, half] + wide_dot(s_pair, rhs[:, half] - applied))
    twice = jnp.concatenate(twice, axis=1)

    lanes = lax.broadcasted_iota(jnp.int32, (64, 128), 1)

    def eights(x, first):
        mine = left_by(x, first)[:, :128] if first else x[:, :128]
        return jnp.where(lanes < 8, mine, left_by(x, 120 + first)[:, :128])

    held = eights(twice, 64)
    applied = couple([eights(twice, 8 * k) for k in range(8)], table[24:32, :128], held, matrix)
    correction = held + wide_dot(s_pair, eights(rhs, 64) - applied)

    b_pair = back_pair[...]
    from_left = left[184:192].astype(jnp.int32)
    from_right = right[184:192].astype(jnp.int32)
    theirs = jnp.where(group == 0, from_left, from_right)

    def shift(slots, by):
        return jnp.where(slots < 0, -1, slots + by)

    three = prolong(correction, table[0:1], table[1:2], b_pair)
    two = prolong(
        three,
        jnp.concatenate([table[5:6, :128], shift(theirs[4:5], 128)], axis=1),
        jnp.concatenate([table[6:7, :128], theirs[5:6]], axis=1),
        b_pair,
    )
    lane = lax.broadcasted_iota(jnp.int32, (8, 128), 1)
    left_slots = shift(from_left, jnp.where(group == 0, 128, 0))
    right_slots = shift(from_right, jnp.where(group == 7, 128, 0))
    mine = pltpu.roll(table[0:8, :128], 64, axis=1)
    one = prolong(
        two,
        jnp.concatenate(
            [jnp.where(lane < 64, left_slots[2:3], mine[3:4])[0:1], right_slots[2:3]], axis=1
        ),
        jnp.concatenate(
            [jnp.where(lane < 64, from_left[3:4], mine[4:5])[0:1], from_right[3:4]], axis=1
        ),
        b_pair,
    )
    zero = prolong(
        one,
        jnp.concatenate([from_left[0:1], owners_zero[0:1] + 64, from_right[0:1] + 128], axis=1),
        jnp.concatenate([from_left[1:2], owners_zero[1:2], from_right[1:2]], axis=1),
        b_pair,
    )
    window[...] = iterate[...] + left_by(zero, 64)[:, :384]

    for at in range(2):
        columns = slice(128 * at, 128 * at + 128)
        applied, held, rhs, levels = fine_step(
            window[:, 128 * at : 128 * at + 256], facts[:, columns], matrix
        )
        out[:, columns] = held + wide_dot(s_pair, rhs * power(levels) - applied)


def call(kernel, outs, scratch, name, flops, places, *args, limit=VMEM_LIMIT):
    spaces = {
        "s": pl.BlockSpec(memory_space=pltpu.SMEM),
        "v": pl.BlockSpec(memory_space=pltpu.VMEM),
        "h": pl.BlockSpec(memory_space=pltpu.HBM),
    }
    fetched = [at for at, place in enumerate(places) if place == "h"]

    def body(*refs):
        inputs = list(refs[: len(args)])
        rest = refs[len(args) :]
        if fetched:
            targets, arrived = rest[len(outs) : len(outs) + len(fetched)], rest[-1]
            rest = rest[: len(outs)] + rest[len(outs) + len(fetched) : -1]
            copies = [
                pltpu.make_async_copy(inputs[at], target, arrived.at[which])
                for which, (at, target) in enumerate(zip(fetched, targets))
            ]
            for copy in copies:
                copy.start()
            for copy in copies:
                copy.wait()
            for at, target in zip(fetched, targets):
                inputs[at] = target
        kernel(*inputs, *rest)

    shapes = [pltpu.VMEM(args[at].shape, args[at].dtype) for at in fetched]
    shapes += [pltpu.VMEM(shape, dtype) for shape, dtype in scratch]
    if fetched:
        shapes.append(pltpu.SemaphoreType.DMA((len(fetched),)))
    return pl.pallas_call(
        body,
        out_shape=[jax.ShapeDtypeStruct(shape, dtype) for shape, dtype in outs],
        in_specs=[spaces[place] for place in places],
        out_specs=[spaces["v"]] * len(outs),
        scratch_shapes=shapes,
        compiler_params=pltpu.CompilerParams(vmem_limit_bytes=limit),
        cost_estimate=pl.CostEstimate(flops=flops, bytes_accessed=1 << 20, transcendentals=0),
        name=name,
    )(*args)


AXES = ("curve", "group")


def both_ways(up_part, down_part):
    peers = lax.axis_size(AXES)
    up = [(i, i + 1) for i in range(peers - 1)]
    down = [(i + 1, i) for i in range(peers - 1)]
    return lax.ppermute(up_part, AXES, up), lax.ppermute(down_part, AXES, down)


DEPTH = 32
WIDTH = 4


def spread(x, axis, count, groups=None):
    copies = jnp.broadcast_to(x[None], (count,) + x.shape)
    return lax.all_to_all(copies, axis, 0, 0, axis_index_groups=groups)


def share_coarse(part):
    along_z = [[x * DEPTH + z for z in range(DEPTH)] for x in range(WIDTH)]
    along_x = [[x * DEPTH + z for x in range(WIDTH)] for z in range(DEPTH)]
    total = jnp.sum(spread(part, "group", 8), axis=0)
    column = spread(total, "curve", DEPTH, along_z)
    return spread(column, "curve", WIDTH, along_x)


def stage_pack(*args):
    outs = (
        ((192, 128), F32),
        ((192, 128), F32),
        ((64, 256), F32),
        ((88, 256), F32),
        ((8, 256), jnp.int32),
    )
    return call(pack_kernel, outs, (), "pack", 1 << 20, "shhhhhhhh", *args, limit=PACK_LIMIT)


def stage_prepare(*args):
    outs = (
        ((128, 2048), BF16),
        ((128, 64), BF16),
        ((128, 512), BF16),
        ((128, 512), BF16),
        ((40, 256), jnp.int32),
    )
    return call(prepare_kernel, outs, (), "prepare", 1 << 20, "svvvvvvvvvv", *args)


def stage_before(*args):
    outs = (((64, 384), F32), ((4, 128), F32))
    scratch = (
        ((64, 640), F32),
        ((64, 512), F32),
        ((88, 512), F32),
        ((88, 384), F32),
        ((64, 256), F32),
    )
    return call(before_kernel, outs, scratch, "before", 1 << 31, "v" * 9, *args)


def stage_finish(*args):
    outs = (((64, 256), F32),)
    return call(
        finish_kernel, outs, (((64, 384), F32),), "finish", 1 << 30, "s" + "v" * 10, *args
    )


def shards(
    right_side,
    start_field,
    block_level,
    neighbors,
    neighbor_kinds,
    owners_zero,
    owners_one,
    owners_two,
    owners_three,
    coarse_neighbors,
    coarse_kinds,
    coarse_level,
    stiffness,
    smoother,
    couplings,
    restriction,
):
    place = jnp.stack([lax.axis_index("curve"), lax.axis_index("group")]).astype(jnp.int32)
    up, down, field, facts, parents = stage_pack(
        place,
        right_side,
        start_field,
        block_level[None, :],
        neighbors,
        neighbor_kinds,
        owners_zero,
        owners_one,
        owners_two,
    )
    left, right = both_ways(up, down)
    coupling_pair, smoother_pair, restriction_pair, back_pair, table = stage_prepare(
        place,
        couplings,
        stiffness,
        smoother,
        restriction,
        owners_one,
        owners_two,
        owners_three,
        coarse_neighbors,
        coarse_kinds,
        coarse_level[None, :],
    )
    iterate, part = stage_before(
        left,
        field,
        facts,
        right,
        parents,
        coupling_pair,
        smoother_pair,
        restriction_pair,
        table,
    )
    gathered = share_coarse(part)
    gathered = gathered.reshape(-1, gathered.shape[-1])
    (out,) = stage_finish(
        place,
        gathered,
        table,
        left,
        right,
        parents,
        coupling_pair,
        smoother_pair,
        back_pair,
        iterate,
        facts,
    )
    return out


def solution(mesh):
    fine = P(None, ("curve", "group"))
    return jax.shard_map(
        shards,
        mesh=mesh,
        in_specs=(
            fine,
            fine,
            P(("curve", "group")),
            fine,
            fine,
            fine,
            P(None, "curve"),
            P(None, "curve"),
            P(),
            P(),
            P(),
            P(),
            P(),
            P(),
            P(),
            P(),
        ),
        out_specs=fine,
        check_vma=False,
    )
```

```python
import jax
import jax.numpy as jnp
from jax import lax
from jax.experimental import pallas as pl
from jax.experimental.pallas import tpu as pltpu
from jax.sharding import PartitionSpec as P

HALO = 64
DAMPING = 0.7
F32 = jnp.float32
BF16 = jnp.bfloat16
VMEM_LIMIT = 40 * 1024 * 1024
PACK_LIMIT = 60 * 1024 * 1024


def halves(x):
    high = x.astype(BF16)
    return high, (x - high.astype(F32)).astype(BF16)


def nn(a, b):
    return lax.dot_general(a, b, (((1,), (0,)), ((), ())), preferred_element_type=F32)


def nt(a, b):
    return lax.dot_general(a, b, (((1,), (1,)), ((), ())), preferred_element_type=F32)


def corners(product):
    half = product.shape[1] // 2
    top, low = product[:64], product[64:]
    return top[:, :half] + (top[:, half:] + low[:, :half]) + low[:, half:]


def wide_dot(matrix_pair, x):
    high, low = halves(x)
    return corners(nn(matrix_pair, jnp.concatenate([high, low], axis=1)))


def stacked(x):
    return jnp.concatenate(halves(x), axis=0)


def folded(x):
    half = x.shape[0] // 2
    return x[:half] + x[half:]


def onehot_rows(row_count, columns):
    rows = lax.broadcasted_iota(jnp.int32, (row_count, columns.shape[1]), 0)
    return jnp.where(rows == columns, 1.0, 0.0).astype(BF16)


def left_by(x, lanes):
    size = x.shape[1]
    return pltpu.roll(x, (size - lanes) % size, axis=1)


def couple(values, kinds, own, coupling_pair):
    values = [v.reshape(8, 8, 128) for v in values]
    marks = [jnp.broadcast_to(kinds[slot : slot + 1], (8, 128)) for slot in range(8)]
    for slot in range(8):
        for later in range(slot + 1, 8):
            same = marks[later] == marks[slot]
            values[slot] = values[slot] + jnp.where(same[None], values[later], 0.0)
            marks[later] = jnp.where(same, -1 - later, marks[later])
    parts = []
    for value in values:
        high, low = halves(value.reshape(64, 128))
        parts.append([half[16 * at : 16 * at + 16] for half in (high, low) for at in range(4)])
    tags = [jnp.concatenate([mark, mark], axis=0).astype(jnp.int16) for mark in marks]
    none = jnp.zeros((16, 128), BF16)
    total = None
    for part in range(8):
        pieces = []
        for kind in range(4 * part, 4 * part + 4):
            if kind < 30:
                chosen = [none] * 8
                for slot in range(8):
                    hit = tags[slot] == jnp.asarray(kind, jnp.int16)
                    chosen = [jnp.where(hit, new, old) for new, old in zip(parts[slot], chosen)]
                high = jnp.concatenate(chosen[:4], axis=0)
                low = jnp.concatenate(chosen[4:], axis=0)
            elif kind == 30:
                high, low = halves(own)
            else:
                high = low = jnp.zeros((64, 128), BF16)
            pieces.append(jnp.concatenate([high, low], axis=1))
        block = jnp.concatenate(pieces, axis=0)
        product = nn(coupling_pair[:, 256 * part : 256 * part + 256], block)
        total = product if total is None else total + product
    return corners(total)


def fine_tile(window, offsets, kinds, coupling_pair):
    lanes = lax.broadcasted_iota(jnp.int32, offsets.shape, 1)
    targets = jnp.where(offsets != 0, lanes + offsets + HALO, -1)
    window_pair = stacked(window)
    values = []
    for slot in range(0, 8, 2):
        columns = jnp.concatenate([targets[slot : slot + 1], targets[slot + 1 : slot + 2]], axis=1)
        picked = folded(nn(window_pair, onehot_rows(256, columns)))
        values += [picked[:, :128], picked[:, 128:]]
    own = left_by(window, HALO)[:, :128]
    return couple(values, kinds, own, coupling_pair), own


def by_octant(x, octant):
    return jnp.concatenate([jnp.where(octant == which, x, 0.0) for which in range(8)], axis=0)


def restrict(x, slot, octant, restriction_pair, parents):
    mapped = wide_dot(restriction_pair, by_octant(x, octant))
    return folded(nt(stacked(mapped), onehot_rows(parents, slot)))


def prolong(x, slot, octant, back_pair):
    pulled = folded(nn(stacked(x), onehot_rows(x.shape[1], slot)))
    return wide_dot(back_pair, by_octant(pulled, octant))


def power(levels):
    return jnp.left_shift(jnp.ones_like(levels), levels).astype(F32)


def inverse_power(levels):
    return jnp.where(levels == 0, 1.0, jnp.where(levels == 1, 0.5, jnp.where(levels == 2, 0.25, 0.125)))


def position():
    return lax.axis_index("curve"), lax.axis_index("group")


def own_lanes(ref, rows, block, per):
    share = 128 // per
    first = pl.multiple_of((block // share) * 128, 128)
    held = ref[rows, pl.ds(first, 128)]
    held = jnp.broadcast_to(held, (8, 128))
    if share > 1:
        held = pltpu.roll(held, lax.rem(128 - per * lax.rem(block, share), 128), axis=1)
    lanes = lax.broadcasted_iota(jnp.int32, (8, 128), 1)
    return jnp.where(lanes < per, held, -1)


def other_curve(member, group):
    return jnp.where(
        group == 0,
        jnp.maximum(member - 1, 0),
        jnp.where(group == 7, jnp.minimum(member + 1, 127), member),
    )


def prepare_kernel(
    couplings,
    stiffness,
    smoother,
    restriction,
    owners_one,
    owners_two,
    owners_three,
    coarse_neighbors,
    coarse_kinds,
    coarse_level,
    coupling_pair,
    smoother_pair,
    restriction_pair,
    back_pair,
    table,
):
    def store(target, first, x):
        high, low = halves(x)
        target[0:64, first : first + x.shape[1]] = high
        target[64:128, first : first + x.shape[1]] = low

    for part in range(15):
        store(
            coupling_pair,
            128 * part,
            jnp.concatenate([couplings[2 * part], couplings[2 * part + 1]], axis=1),
        )
    store(
        coupling_pair,
        1920,
        jnp.concatenate([stiffness[...], jnp.zeros((64, 64), F32)], axis=1),
    )
    store(smoother_pair, 0, DAMPING * smoother[...])
    for part in range(4):
        first, second = restriction[2 * part], restriction[2 * part + 1]
        store(restriction_pair, 128 * part, jnp.concatenate([first, second], axis=1))
        upright = jnp.concatenate([first, second], axis=0)
        square = jnp.concatenate([upright, jnp.zeros((128, 64), F32)], axis=1)
        store(back_pair, 128 * part, jnp.transpose(square)[0:64])

    member, group = position()
    other = other_curve(member, group)
    lanes = lax.broadcasted_iota(jnp.int32, (8, 128), 1)

    def row(at):
        return slice(at, at + 1)

    mine = own_lanes(owners_three, row(0), member, 32)
    theirs = own_lanes(owners_three, row(0), other, 32)
    theirs = jnp.where(theirs < 0, -1, theirs + 8)
    table[0:1] = jnp.concatenate([mine, theirs], axis=1)[0:1]
    table[1:2] = jnp.concatenate(
        [
            own_lanes(owners_three, row(1), member, 32),
            own_lanes(owners_three, row(1), other, 32),
        ],
        axis=1,
    )[0:1]
    level = jnp.maximum(own_lanes(coarse_level, row(0), member, 8), 0)
    zero = jnp.int32(0)
    for at, values in enumerate(
        (
            level,
            own_lanes(owners_one, row(0), group, 64),
            own_lanes(owners_one, row(1), group, 64),
            own_lanes(owners_two, row(0), zero, 128),
            own_lanes(owners_two, row(1), zero, 128),
            jnp.zeros_like(level),
        )
    ):
        table[2 + at : 3 + at] = jnp.concatenate([values, values], axis=1)[0:1]
    every = slice(0, 8)
    near = own_lanes(coarse_neighbors, every, member, 8)
    near_kinds = jnp.where(near >= 0, own_lanes(coarse_kinds, every, member, 8), -1)
    far = own_lanes(coarse_neighbors, every, other, 8)
    far_kinds = jnp.where(far >= 0, own_lanes(coarse_kinds, every, other, 8), -1)
    wanted = jnp.full((8, 128), -1, jnp.int32)
    for slot in range(8):
        for first, blocks in ((8 * slot, near), (64 + 8 * slot, far)):
            moved = pltpu.roll(blocks, first, axis=1) if first else blocks
            moved = jnp.broadcast_to(moved[slot : slot + 1], (8, 128))
            wanted = jnp.where((lanes >= first) & (lanes < first + 8), moved, wanted)
    sixteen = jnp.where(lanes < 8, 8 * member + lanes, 8 * other + lanes - 8)
    sixteen = jnp.where(lanes < 16, sixteen, -1)
    sixteen_kinds = jnp.where(lanes < 8, near_kinds, pltpu.roll(far_kinds, 8, axis=1))
    shifted = coarse_neighbors[...] + 1
    facts = jnp.concatenate(
        [shifted >> 5, shifted & 31, coarse_kinds[...], jnp.zeros_like(shifted)], axis=0
    )
    facts = facts.astype(F32).astype(BF16)
    found = nn(facts, onehot_rows(1024, wanted[0:1])).astype(jnp.int32)
    links = 32 * found[0:8] + found[8:16] - 1
    table[8:16] = jnp.concatenate([links, found[16:24]], axis=1)
    table[16:24] = jnp.concatenate([sixteen_kinds, wanted], axis=1)
    table[24:32] = jnp.concatenate([sixteen, sixteen], axis=1)


def pack_kernel(
    right_side,
    start_field,
    block_level,
    neighbors,
    neighbor_kinds,
    owners_zero,
    owners_one,
    owners_two,
    up,
    down,
    field,
    facts,
    parents,
):
    lane = lax.broadcasted_iota(jnp.int32, (32, 128), 1)
    low, high = start_field[:, 0:128], start_field[:, 128:256]
    up[0:64] = high
    up[64:96] = jnp.where(lane < 64, left_by(low[0:32], 64), low[32:64])
    down[0:64] = low
    down[64:96] = jnp.where(lane < 64, high[0:32], left_by(high[32:64], 64))
    field[...] = start_field[...]
    facts[0:64] = right_side[...]
    facts[64:72] = neighbors[...].astype(F32)
    facts[72:80] = neighbor_kinds[...].astype(F32)
    facts[80:88] = jnp.broadcast_to(block_level[...], (8, 256)).astype(F32)
    parents[...] = jnp.concatenate([owners_zero[...]] * 4, axis=0)
    group = position()[1]
    shared = [
        own_lanes(owners_one, slice(0, 1), group, 64),
        own_lanes(owners_one, slice(1, 2), group, 64),
        jnp.broadcast_to(owners_two[0:1, :], (8, 128)),
        jnp.broadcast_to(owners_two[1:2, :], (8, 128)),
    ]
    for target, columns in ((up, slice(128, 256)), (down, slice(0, 128))):
        target[96:184] = facts[:, columns]
        target[184:186] = owners_zero[:, columns].astype(F32)
        for at, values in enumerate(shared):
            target[186 + at : 187 + at] = values[0:1].astype(F32)
        target[190:192] = jnp.zeros((2, 128), F32)


def fine_step(window, here, coupling_pair):
    offsets = here[64:72].astype(jnp.int32)
    kinds = here[72:80].astype(jnp.int32)
    levels = here[80:81].astype(jnp.int32)
    applied, held = fine_tile(window, offsets, kinds, coupling_pair)
    return applied, held, here[0:64], levels


def before_kernel(
    left,
    start_field,
    facts,
    right,
    owners_zero,
    coupling_pair,
    smoother_pair,
    restriction_pair,
    table,
    iterate_out,
    part_out,
    first,
    second,
    facts_wide,
    facts_narrow,
    remainder,
):
    matrix = coupling_pair
    far_left, far_right = left[64:96], right[64:96]
    row = jnp.concatenate(
        [
            jnp.concatenate([left_by(far_left, 64), far_left], axis=0),
            left[0:64],
            start_field[...],
            right[0:64],
            jnp.concatenate([far_right, left_by(far_right, 64)], axis=0),
        ],
        axis=1,
    )
    first[...] = left_by(row, 64)[:, :640]
    wide = jnp.concatenate([left[96:184], facts[...], right[96:184]], axis=1)
    facts_wide[...] = wide
    facts_narrow[...] = left_by(wide, 64)[:, :384]

    def sweep(source, facts_of, target, tiles):
        for at in range(tiles):
            columns = slice(128 * at, 128 * at + 128)
            applied, held, rhs, levels = fine_step(
                source[:, 128 * at : 128 * at + 256], facts_of[:, columns], matrix[...]
            )
            change = wide_dot(smoother_pair[...], rhs * power(levels) - applied)
            target[:, columns] = held + change

    sweep(first, facts_wide, second, 4)
    sweep(second, facts_narrow, iterate_out, 3)
    for at in range(2):
        columns = slice(128 * at, 128 * at + 128)
        applied, held, rhs, levels = fine_step(
            iterate_out[:, 128 * at : 128 * at + 256], facts[:, columns], matrix[...]
        )
        remainder[:, columns] = rhs - inverse_power(levels) * applied

    r_pair = restriction_pair[...]
    one = restrict(remainder[...], owners_zero[0:1], owners_zero[1:2], r_pair, 128)
    two = restrict(one, table[3:4, :128], table[4:5, :128], r_pair, 128)
    three = restrict(two, table[5:6, :128], table[6:7, :128], r_pair, 128)
    four = restrict(three, table[0:1, :128], table[1:2, :128], r_pair, 128)
    four = four * power(table[2:3, :128])
    both = jnp.concatenate([four, left_by(four, 4)], axis=0)
    part_out[...] = jnp.transpose(both)[0:4]


def finish_kernel(
    gathered,
    table,
    left,
    right,
    owners_zero,
    coupling_pair,
    smoother_pair,
    back_pair,
    iterate,
    facts,
    out,
    window,
):
    group = position()[1]
    field_pair = stacked(jnp.transpose(gathered[...]))
    s_pair = smoother_pair[...]
    matrix = coupling_pair[...]

    def gather(blocks):
        rows = jnp.where(blocks >= 0, 4 * (blocks >> 3) + (blocks & 3), -1)
        both = folded(nn(field_pair, onehot_rows(512, rows)))
        return jnp.where(((blocks >> 2) & 1) == 0, both[0:64], both[64:128])

    columns = [table[8 + slot : 9 + slot, :128] for slot in range(8)]
    columns += [table[16:17, 128:], table[24:25, :128]]
    values, known = [], []
    for at in range(0, 10, 2):
        both = gather(jnp.concatenate(columns[at : at + 2], axis=1))
        swept = wide_dot(s_pair, both)
        values += [swept[:, :128], swept[:, 128:]]
        known += [both[:, :128], both[:, 128:]]
    rhs, own_rhs = known[8:]
    once, own_once = values[8:]

    lanes = lax.broadcasted_iota(jnp.int32, (64, 128), 1)

    def eights(x, slot):
        mine = left_by(x, 8 * slot) if slot else x
        return jnp.where(lanes < 8, mine, left_by(x, 56 + 8 * slot))

    kinds = table[16:24, :128]
    applied = couple(values[:8], table[8:16, 128:], once, matrix)
    twice = once + wide_dot(s_pair, rhs - applied)
    applied = couple([eights(once, slot) for slot in range(8)], kinds, own_once, matrix)
    own_twice = own_once + wide_dot(s_pair, own_rhs - applied)
    applied = couple([eights(twice, slot) for slot in range(8)], kinds, own_twice, matrix)
    correction = own_twice + wide_dot(s_pair, own_rhs - applied)

    b_pair = back_pair[...]
    from_left = left[184:192].astype(jnp.int32)
    from_right = right[184:192].astype(jnp.int32)
    theirs = jnp.where(group == 0, from_left, from_right)

    def shift(slots, by):
        return jnp.where(slots < 0, -1, slots + by)

    three = prolong(correction, table[0:1], table[1:2], b_pair)
    two = prolong(
        three,
        jnp.concatenate([table[5:6, :128], shift(theirs[4:5], 128)], axis=1),
        jnp.concatenate([table[6:7, :128], theirs[5:6]], axis=1),
        b_pair,
    )
    lane = lax.broadcasted_iota(jnp.int32, (8, 128), 1)
    left_slots = shift(from_left, jnp.where(group == 0, 128, 0))
    right_slots = shift(from_right, jnp.where(group == 7, 128, 0))
    mine = pltpu.roll(table[0:8, :128], 64, axis=1)
    one = prolong(
        two,
        jnp.concatenate(
            [jnp.where(lane < 64, left_slots[2:3], mine[3:4])[0:1], right_slots[2:3]], axis=1
        ),
        jnp.concatenate(
            [jnp.where(lane < 64, from_left[3:4], mine[4:5])[0:1], from_right[3:4]], axis=1
        ),
        b_pair,
    )
    zero = prolong(
        one,
        jnp.concatenate([from_left[0:1], owners_zero[0:1] + 64, from_right[0:1] + 128], axis=1),
        jnp.concatenate([from_left[1:2], owners_zero[1:2], from_right[1:2]], axis=1),
        b_pair,
    )
    window[...] = iterate[...] + left_by(zero, 64)[:, :384]

    for at in range(2):
        columns = slice(128 * at, 128 * at + 128)
        applied, held, rhs, levels = fine_step(
            window[:, 128 * at : 128 * at + 256], facts[:, columns], matrix
        )
        out[:, columns] = held + wide_dot(s_pair, rhs * power(levels) - applied)


def call(kernel, outs, scratch, name, flops, places, *args, limit=VMEM_LIMIT):
    spaces = {
        "s": pl.BlockSpec(memory_space=pltpu.SMEM),
        "v": pl.BlockSpec(memory_space=pltpu.VMEM),
        "h": pl.BlockSpec(memory_space=pltpu.HBM),
    }
    fetched = [at for at, place in enumerate(places) if place == "h"]

    def body(*refs):
        inputs = list(refs[: len(args)])
        rest = refs[len(args) :]
        if fetched:
            targets, arrived = rest[len(outs) : len(outs) + len(fetched)], rest[-1]
            rest = rest[: len(outs)] + rest[len(outs) + len(fetched) : -1]
            copies = [
                pltpu.make_async_copy(inputs[at], target, arrived.at[which])
                for which, (at, target) in enumerate(zip(fetched, targets))
            ]
            for copy in copies:
                copy.start()
            for copy in copies:
                copy.wait()
            for at, target in zip(fetched, targets):
                inputs[at] = target
        kernel(*inputs, *rest)

    shapes = [pltpu.VMEM(args[at].shape, args[at].dtype) for at in fetched]
    shapes += [pltpu.VMEM(shape, dtype) for shape, dtype in scratch]
    if fetched:
        shapes.append(pltpu.SemaphoreType.DMA((len(fetched),)))
    return pl.pallas_call(
        body,
        out_shape=[jax.ShapeDtypeStruct(shape, dtype) for shape, dtype in outs],
        in_specs=[spaces[place] for place in places],
        out_specs=[spaces["v"]] * len(outs),
        scratch_shapes=shapes,
        compiler_params=pltpu.CompilerParams(vmem_limit_bytes=limit),
        cost_estimate=pl.CostEstimate(flops=flops, bytes_accessed=1 << 20, transcendentals=0),
        name=name,
    )(*args)


AXES = ("curve", "group")


def both_ways(up_part, down_part):
    peers = lax.axis_size(AXES)
    up = [(i, i + 1) for i in range(peers - 1)]
    down = [(i + 1, i) for i in range(peers - 1)]
    return lax.ppermute(up_part, AXES, up), lax.ppermute(down_part, AXES, down)


DEPTH = 32
WIDTH = 4


def spread(x, axis, count, groups=None):
    copies = jnp.broadcast_to(x[None], (count,) + x.shape)
    return lax.all_to_all(copies, axis, 0, 0, axis_index_groups=groups)


def share_coarse(part):
    along_z = [[x * DEPTH + z for z in range(DEPTH)] for x in range(WIDTH)]
    along_x = [[x * DEPTH + z for x in range(WIDTH)] for z in range(DEPTH)]
    total = jnp.sum(spread(part, "group", 8), axis=0)
    column = spread(total, "curve", DEPTH, along_z)
    return spread(column, "curve", WIDTH, along_x)


def stage_pack(*args):
    outs = (
        ((192, 128), F32),
        ((192, 128), F32),
        ((64, 256), F32),
        ((88, 256), F32),
        ((8, 256), jnp.int32),
    )
    return call(pack_kernel, outs, (), "pack", 1 << 20, "hhhhhhhh", *args, limit=PACK_LIMIT)


def stage_prepare(*args):
    outs = (
        ((128, 2048), BF16),
        ((128, 64), BF16),
        ((128, 512), BF16),
        ((128, 512), BF16),
        ((32, 256), jnp.int32),
    )
    return call(prepare_kernel, outs, (), "prepare", 1 << 20, "vvvvvvvvvv", *args)


def stage_before(*args):
    outs = (((64, 384), F32), ((4, 128), F32))
    scratch = (
        ((64, 640), F32),
        ((64, 512), F32),
        ((88, 512), F32),
        ((88, 384), F32),
        ((64, 256), F32),
    )
    return call(before_kernel, outs, scratch, "before", 1 << 31, "v" * 9, *args)


def stage_finish(*args):
    outs = (((64, 256), F32),)
    return call(
        finish_kernel, outs, (((64, 384), F32),), "finish", 1 << 30, "v" * 10, *args
    )


def shards(
    right_side,
    start_field,
    block_level,
    neighbors,
    neighbor_kinds,
    owners_zero,
    owners_one,
    owners_two,
    owners_three,
    coarse_neighbors,
    coarse_kinds,
    coarse_level,
    stiffness,
    smoother,
    couplings,
    restriction,
):
    up, down, field, facts, parents = stage_pack(
        right_side,
        start_field,
        block_level[None, :],
        neighbors,
        neighbor_kinds,
        owners_zero,
        owners_one,
        owners_two,
    )
    left, right = both_ways(up, down)
    coupling_pair, smoother_pair, restriction_pair, back_pair, table = stage_prepare(
        couplings,
        stiffness,
        smoother,
        restriction,
        owners_one,
        owners_two,
        owners_three,
        coarse_neighbors,
        coarse_kinds,
        coarse_level[None, :],
    )
    iterate, part = stage_before(
        left,
        field,
        facts,
        right,
        parents,
        coupling_pair,
        smoother_pair,
        restriction_pair,
        table,
    )
    gathered = share_coarse(part)
    gathered = gathered.reshape(-1, gathered.shape[-1])
    (out,) = stage_finish(
        gathered,
        table,
        left,
        right,
        parents,
        coupling_pair,
        smoother_pair,
        back_pair,
        iterate,
        facts,
    )
    return out


def solution(mesh):
    fine = P(None, ("curve", "group"))
    return jax.shard_map(
        shards,
        mesh=mesh,
        in_specs=(
            fine,
            fine,
            P(("curve", "group")),
            fine,
            fine,
            fine,
            P(None, "curve"),
            P(None, "curve"),
            P(),
            P(),
            P(),
            P(),
            P(),
            P(),
            P(),
            P(),
        ),
        out_specs=fine,
        check_vma=False,
    )
```

```python
import jax
import jax.numpy as jnp
from jax import lax
from jax.experimental import pallas as pl
from jax.experimental.pallas import tpu as pltpu
from jax.sharding import PartitionSpec as P

HALO = 64
DAMPING = 0.7
F32 = jnp.float32
BF16 = jnp.bfloat16
VMEM_LIMIT = 40 * 1024 * 1024
PACK_LIMIT = 60 * 1024 * 1024


def halves(x):
    high = x.astype(BF16)
    return high, (x - high.astype(F32)).astype(BF16)


def nn(a, b):
    return lax.dot_general(a, b, (((1,), (0,)), ((), ())), preferred_element_type=F32)


def nt(a, b):
    return lax.dot_general(a, b, (((1,), (1,)), ((), ())), preferred_element_type=F32)


def corners(product):
    half = product.shape[1] // 2
    top, low = product[:64], product[64:]
    return top[:, :half] + (top[:, half:] + low[:, :half]) + low[:, half:]


def wide_dot(matrix_pair, x):
    high, low = halves(x)
    return corners(nn(matrix_pair, jnp.concatenate([high, low], axis=1)))


def stacked(x):
    return jnp.concatenate(halves(x), axis=0)


def folded(x):
    half = x.shape[0] // 2
    return x[:half] + x[half:]


def onehot_rows(row_count, columns):
    rows = lax.broadcasted_iota(jnp.int32, (row_count, columns.shape[1]), 0)
    return jnp.where(rows == columns, 1.0, 0.0).astype(BF16)


def left_by(x, lanes):
    size = x.shape[1]
    return pltpu.roll(x, (size - lanes) % size, axis=1)


def couple(values, kinds, own, coupling_pair):
    values = [v.reshape(8, 8, 128) for v in values]
    marks = [jnp.broadcast_to(kinds[slot : slot + 1], (8, 128)) for slot in range(8)]
    for slot in range(8):
        for later in range(slot + 1, 8):
            same = marks[later] == marks[slot]
            values[slot] = values[slot] + jnp.where(same[None], values[later], 0.0)
            marks[later] = jnp.where(same, -1 - later, marks[later])
    parts = []
    for value in values:
        high, low = halves(value.reshape(64, 128))
        parts.append([half[16 * at : 16 * at + 16] for half in (high, low) for at in range(4)])
    tags = [jnp.concatenate([mark, mark], axis=0).astype(jnp.int16) for mark in marks]
    none = jnp.zeros((16, 128), BF16)
    total = None
    for part in range(8):
        pieces = []
        for kind in range(4 * part, 4 * part + 4):
            if kind < 30:
                chosen = [none] * 8
                for slot in range(8):
                    hit = tags[slot] == jnp.asarray(kind, jnp.int16)
                    chosen = [jnp.where(hit, new, old) for new, old in zip(parts[slot], chosen)]
                high = jnp.concatenate(chosen[:4], axis=0)
                low = jnp.concatenate(chosen[4:], axis=0)
            elif kind == 30:
                high, low = halves(own)
            else:
                high = low = jnp.zeros((64, 128), BF16)
            pieces.append(jnp.concatenate([high, low], axis=1))
        block = jnp.concatenate(pieces, axis=0)
        product = nn(coupling_pair[:, 256 * part : 256 * part + 256], block)
        total = product if total is None else total + product
    return corners(total)


def look_up(window, offsets):
    lanes = lax.broadcasted_iota(jnp.int32, offsets.shape, 1)
    targets = jnp.where(offsets != 0, lanes + offsets + HALO, -1)
    window_pair = stacked(window)
    values = []
    for slot in range(0, 8, 2):
        columns = jnp.concatenate([targets[slot : slot + 1], targets[slot + 1 : slot + 2]], axis=1)
        picked = folded(nn(window_pair, onehot_rows(256, columns)))
        values += [picked[:, :128], picked[:, 128:]]
    return values, left_by(window, HALO)[:, :128]


def by_octant(x, octant):
    return jnp.concatenate([jnp.where(octant == which, x, 0.0) for which in range(8)], axis=0)


def restrict(x, slot, octant, restriction_pair, parents):
    mapped = wide_dot(restriction_pair, by_octant(x, octant))
    return folded(nt(stacked(mapped), onehot_rows(parents, slot)))


def prolong(x, slot, octant, back_pair):
    pulled = folded(nn(stacked(x), onehot_rows(x.shape[1], slot)))
    return wide_dot(back_pair, by_octant(pulled, octant))


def power(levels):
    return jnp.left_shift(jnp.ones_like(levels), levels).astype(F32)


def inverse_power(levels):
    return jnp.where(levels == 0, 1.0, jnp.where(levels == 1, 0.5, jnp.where(levels == 2, 0.25, 0.125)))


def position():
    return lax.axis_index("curve"), lax.axis_index("group")


def own_lanes(ref, rows, block, per):
    share = 128 // per
    first = pl.multiple_of((block // share) * 128, 128)
    held = ref[rows, pl.ds(first, 128)]
    held = jnp.broadcast_to(held, (8, 128))
    if share > 1:
        held = pltpu.roll(held, lax.rem(128 - per * lax.rem(block, share), 128), axis=1)
    lanes = lax.broadcasted_iota(jnp.int32, (8, 128), 1)
    return jnp.where(lanes < per, held, -1)


def other_curve(member, group):
    return jnp.where(
        group == 0,
        jnp.maximum(member - 1, 0),
        jnp.where(group == 7, jnp.minimum(member + 1, 127), member),
    )


def prepare_kernel(
    couplings,
    stiffness,
    smoother,
    restriction,
    owners_one,
    owners_two,
    owners_three,
    coarse_neighbors,
    coarse_kinds,
    coarse_level,
    coupling_pair,
    smoother_pair,
    restriction_pair,
    back_pair,
    table,
):
    def store(target, first, x):
        high, low = halves(x)
        target[0:64, first : first + x.shape[1]] = high
        target[64:128, first : first + x.shape[1]] = low

    for part in range(15):
        store(
            coupling_pair,
            128 * part,
            jnp.concatenate([couplings[2 * part], couplings[2 * part + 1]], axis=1),
        )
    store(
        coupling_pair,
        1920,
        jnp.concatenate([stiffness[...], jnp.zeros((64, 64), F32)], axis=1),
    )
    store(smoother_pair, 0, DAMPING * smoother[...])
    for part in range(4):
        first, second = restriction[2 * part], restriction[2 * part + 1]
        store(restriction_pair, 128 * part, jnp.concatenate([first, second], axis=1))
        upright = jnp.concatenate([first, second], axis=0)
        square = jnp.concatenate([upright, jnp.zeros((128, 64), F32)], axis=1)
        store(back_pair, 128 * part, jnp.transpose(square)[0:64])

    member, group = position()
    other = other_curve(member, group)
    lanes = lax.broadcasted_iota(jnp.int32, (8, 128), 1)

    def row(at):
        return slice(at, at + 1)

    mine = own_lanes(owners_three, row(0), member, 32)
    theirs = own_lanes(owners_three, row(0), other, 32)
    theirs = jnp.where(theirs < 0, -1, theirs + 8)
    table[0:1] = jnp.concatenate([mine, theirs], axis=1)[0:1]
    table[1:2] = jnp.concatenate(
        [
            own_lanes(owners_three, row(1), member, 32),
            own_lanes(owners_three, row(1), other, 32),
        ],
        axis=1,
    )[0:1]
    level = jnp.maximum(own_lanes(coarse_level, row(0), member, 8), 0)
    zero = jnp.int32(0)
    for at, values in enumerate(
        (
            level,
            own_lanes(owners_one, row(0), group, 64),
            own_lanes(owners_one, row(1), group, 64),
            own_lanes(owners_two, row(0), zero, 128),
            own_lanes(owners_two, row(1), zero, 128),
            jnp.zeros_like(level),
        )
    ):
        table[2 + at : 3 + at] = jnp.concatenate([values, values], axis=1)[0:1]
    every = slice(0, 8)
    near = own_lanes(coarse_neighbors, every, member, 8)
    near_kinds = jnp.where(near >= 0, own_lanes(coarse_kinds, every, member, 8), -1)
    far = own_lanes(coarse_neighbors, every, other, 8)
    far_kinds = jnp.where(far >= 0, own_lanes(coarse_kinds, every, other, 8), -1)
    wanted = jnp.full((8, 128), -1, jnp.int32)
    for slot in range(8):
        for first, blocks in ((8 * slot, near), (64 + 8 * slot, far)):
            moved = pltpu.roll(blocks, first, axis=1) if first else blocks
            moved = jnp.broadcast_to(moved[slot : slot + 1], (8, 128))
            wanted = jnp.where((lanes >= first) & (lanes < first + 8), moved, wanted)
    sixteen = jnp.where(lanes < 8, 8 * member + lanes, 8 * other + lanes - 8)
    sixteen = jnp.where(lanes < 16, sixteen, -1)
    sixteen_kinds = jnp.where(lanes < 8, near_kinds, pltpu.roll(far_kinds, 8, axis=1))
    shifted = coarse_neighbors[...] + 1
    facts = jnp.concatenate(
        [shifted >> 5, shifted & 31, coarse_kinds[...], jnp.zeros_like(shifted)], axis=0
    )
    facts = facts.astype(F32).astype(BF16)
    found = nn(facts, onehot_rows(1024, wanted[0:1])).astype(jnp.int32)
    links = 32 * found[0:8] + found[8:16] - 1
    table[8:16] = jnp.concatenate([links, found[16:24]], axis=1)
    table[16:24] = jnp.concatenate([sixteen_kinds, wanted], axis=1)
    table[24:32] = jnp.concatenate([sixteen, sixteen], axis=1)


def pack_kernel(
    right_side,
    start_field,
    block_level,
    neighbors,
    neighbor_kinds,
    owners_zero,
    owners_one,
    owners_two,
    up,
    down,
    field,
    facts,
    parents,
):
    lane = lax.broadcasted_iota(jnp.int32, (32, 128), 1)
    low, high = start_field[:, 0:128], start_field[:, 128:256]
    up[0:64] = high
    up[64:96] = jnp.where(lane < 64, left_by(low[0:32], 64), low[32:64])
    down[0:64] = low
    down[64:96] = jnp.where(lane < 64, high[0:32], left_by(high[32:64], 64))
    field[...] = start_field[...]
    facts[0:64] = right_side[...]
    facts[64:72] = neighbors[...].astype(F32)
    facts[72:80] = neighbor_kinds[...].astype(F32)
    facts[80:88] = jnp.broadcast_to(block_level[...], (8, 256)).astype(F32)
    parents[...] = jnp.concatenate([owners_zero[...]] * 4, axis=0)
    group = position()[1]
    shared = [
        own_lanes(owners_one, slice(0, 1), group, 64),
        own_lanes(owners_one, slice(1, 2), group, 64),
        jnp.broadcast_to(owners_two[0:1, :], (8, 128)),
        jnp.broadcast_to(owners_two[1:2, :], (8, 128)),
    ]
    for target, columns in ((up, slice(128, 256)), (down, slice(0, 128))):
        target[96:184] = facts[:, columns]
        target[184:186] = owners_zero[:, columns].astype(F32)
        for at, values in enumerate(shared):
            target[186 + at : 187 + at] = values[0:1].astype(F32)
        target[190:192] = jnp.zeros((2, 128), F32)


def fine_image(source, facts, tiles, coupling_pair):
    found = []
    applied = []
    for at in range(tiles):
        here = facts[64:72, 128 * at : 128 * at + 128].astype(jnp.int32)
        found.append(look_up(source[:, 128 * at : 128 * at + 256], here))
        values, own = found[-1]
        kinds = facts[72:80, 128 * at : 128 * at + 128].astype(jnp.int32)
        applied.append(couple(values, kinds, own, coupling_pair))
    held = jnp.concatenate([own for _, own in found], axis=1)
    columns = slice(0, 128 * tiles)
    return (
        jnp.concatenate(applied, axis=1),
        held,
        facts[0:64, columns],
        facts[80:81, columns].astype(jnp.int32),
    )


def before_kernel(
    left,
    start_field,
    facts,
    right,
    owners_zero,
    coupling_pair,
    smoother_pair,
    restriction_pair,
    table,
    iterate_out,
    part_out,
    first,
    second,
    facts_wide,
    facts_narrow,
    remainder,
):
    matrix = coupling_pair
    far_left, far_right = left[64:96], right[64:96]
    row = jnp.concatenate(
        [
            jnp.concatenate([left_by(far_left, 64), far_left], axis=0),
            left[0:64],
            start_field[...],
            right[0:64],
            jnp.concatenate([far_right, left_by(far_right, 64)], axis=0),
        ],
        axis=1,
    )
    first[...] = left_by(row, 64)[:, :640]
    wide = jnp.concatenate([left[96:184], facts[...], right[96:184]], axis=1)
    facts_wide[...] = wide
    facts_narrow[...] = left_by(wide, 64)[:, :384]

    def sweep(source, facts_of, target, tiles):
        applied, held, rhs, levels = fine_image(source, facts_of, tiles, matrix)
        change = wide_dot(smoother_pair[...], rhs * power(levels) - applied)
        target[...] = held + change

    sweep(first, facts_wide, second, 4)
    sweep(second, facts_narrow, iterate_out, 3)
    applied, held, rhs, levels = fine_image(iterate_out, facts, 2, matrix)
    remainder[...] = rhs - inverse_power(levels) * applied

    r_pair = restriction_pair[...]
    one = restrict(remainder[...], owners_zero[0:1], owners_zero[1:2], r_pair, 128)
    two = restrict(one, table[3:4, :128], table[4:5, :128], r_pair, 128)
    three = restrict(two, table[5:6, :128], table[6:7, :128], r_pair, 128)
    four = restrict(three, table[0:1, :128], table[1:2, :128], r_pair, 128)
    four = four * power(table[2:3, :128])
    both = jnp.concatenate([four, left_by(four, 4)], axis=0)
    part_out[...] = jnp.transpose(both)[0:4]


def finish_kernel(
    gathered,
    table,
    left,
    right,
    owners_zero,
    coupling_pair,
    smoother_pair,
    back_pair,
    iterate,
    facts,
    out,
    window,
):
    group = position()[1]
    field_pair = stacked(jnp.transpose(gathered[...]))
    s_pair = smoother_pair[...]
    matrix = coupling_pair[...]

    def gather(blocks):
        rows = jnp.where(blocks >= 0, 4 * (blocks >> 3) + (blocks & 3), -1)
        both = folded(nn(field_pair, onehot_rows(512, rows)))
        return jnp.where(((blocks >> 2) & 1) == 0, both[0:64], both[64:128])

    columns = [table[8 + slot : 9 + slot, :128] for slot in range(8)]
    columns += [table[16:17, 128:], table[24:25, :128]]
    values, known = [], []
    for at in range(0, 10, 2):
        both = gather(jnp.concatenate(columns[at : at + 2], axis=1))
        swept = wide_dot(s_pair, both)
        values += [swept[:, :128], swept[:, 128:]]
        known += [both[:, :128], both[:, 128:]]
    rhs, own_rhs = known[8:]
    once, own_once = values[8:]

    lanes = lax.broadcasted_iota(jnp.int32, (64, 128), 1)

    def eights(x, slot):
        mine = left_by(x, 8 * slot) if slot else x
        return jnp.where(lanes < 8, mine, left_by(x, 56 + 8 * slot))

    kinds = table[16:24, :128]
    applied = couple(values[:8], table[8:16, 128:], once, matrix)
    twice = once + wide_dot(s_pair, rhs - applied)
    applied = couple([eights(once, slot) for slot in range(8)], kinds, own_once, matrix)
    own_twice = own_once + wide_dot(s_pair, own_rhs - applied)
    applied = couple([eights(twice, slot) for slot in range(8)], kinds, own_twice, matrix)
    correction = own_twice + wide_dot(s_pair, own_rhs - applied)

    b_pair = back_pair[...]
    from_left = left[184:192].astype(jnp.int32)
    from_right = right[184:192].astype(jnp.int32)
    theirs = jnp.where(group == 0, from_left, from_right)

    def shift(slots, by):
        return jnp.where(slots < 0, -1, slots + by)

    three = prolong(correction, table[0:1], table[1:2], b_pair)
    two = prolong(
        three,
        jnp.concatenate([table[5:6, :128], shift(theirs[4:5], 128)], axis=1),
        jnp.concatenate([table[6:7, :128], theirs[5:6]], axis=1),
        b_pair,
    )
    lane = lax.broadcasted_iota(jnp.int32, (8, 128), 1)
    left_slots = shift(from_left, jnp.where(group == 0, 128, 0))
    right_slots = shift(from_right, jnp.where(group == 7, 128, 0))
    mine = pltpu.roll(table[0:8, :128], 64, axis=1)
    one = prolong(
        two,
        jnp.concatenate(
            [jnp.where(lane < 64, left_slots[2:3], mine[3:4])[0:1], right_slots[2:3]], axis=1
        ),
        jnp.concatenate(
            [jnp.where(lane < 64, from_left[3:4], mine[4:5])[0:1], from_right[3:4]], axis=1
        ),
        b_pair,
    )
    ends_slots = jnp.where(lane < 64, from_right + 128, from_left)[0:1]
    ends_octants = jnp.where(lane < 64, from_right, from_left)[1:2]
    zero = prolong(
        one,
        jnp.concatenate([ends_slots, owners_zero[0:1] + 64], axis=1),
        jnp.concatenate([ends_octants, owners_zero[1:2]], axis=1),
        b_pair,
    )
    zero = jnp.concatenate([zero, zero[:, :128]], axis=1)
    window[...] = iterate[...] + left_by(zero, 64)[:, :384]

    applied, held, rhs, levels = fine_image(window, facts, 2, matrix)
    out[...] = held + wide_dot(s_pair, rhs * power(levels) - applied)


def call(kernel, outs, scratch, name, flops, places, *args, limit=VMEM_LIMIT):
    spaces = {
        "s": pl.BlockSpec(memory_space=pltpu.SMEM),
        "v": pl.BlockSpec(memory_space=pltpu.VMEM),
        "h": pl.BlockSpec(memory_space=pltpu.HBM),
    }
    fetched = [at for at, place in enumerate(places) if place == "h"]

    def body(*refs):
        inputs = list(refs[: len(args)])
        rest = refs[len(args) :]
        if fetched:
            targets, arrived = rest[len(outs) : len(outs) + len(fetched)], rest[-1]
            rest = rest[: len(outs)] + rest[len(outs) + len(fetched) : -1]
            copies = [
                pltpu.make_async_copy(inputs[at], target, arrived.at[which])
                for which, (at, target) in enumerate(zip(fetched, targets))
            ]
            for copy in copies:
                copy.start()
            for copy in copies:
                copy.wait()
            for at, target in zip(fetched, targets):
                inputs[at] = target
        kernel(*inputs, *rest)

    shapes = [pltpu.VMEM(args[at].shape, args[at].dtype) for at in fetched]
    shapes += [pltpu.VMEM(shape, dtype) for shape, dtype in scratch]
    if fetched:
        shapes.append(pltpu.SemaphoreType.DMA((len(fetched),)))
    return pl.pallas_call(
        body,
        out_shape=[jax.ShapeDtypeStruct(shape, dtype) for shape, dtype in outs],
        in_specs=[spaces[place] for place in places],
        out_specs=[spaces["v"]] * len(outs),
        scratch_shapes=shapes,
        compiler_params=pltpu.CompilerParams(vmem_limit_bytes=limit),
        cost_estimate=pl.CostEstimate(flops=flops, bytes_accessed=1 << 20, transcendentals=0),
        name=name,
    )(*args)


AXES = ("curve", "group")


def both_ways(up_part, down_part):
    peers = lax.axis_size(AXES)
    up = [(i, i + 1) for i in range(peers - 1)]
    down = [(i + 1, i) for i in range(peers - 1)]
    return lax.ppermute(up_part, AXES, up), lax.ppermute(down_part, AXES, down)


DEPTH = 32
WIDTH = 4


def spread(x, axis, count, groups=None):
    copies = jnp.broadcast_to(x[None], (count,) + x.shape)
    return lax.all_to_all(copies, axis, 0, 0, axis_index_groups=groups)


def share_coarse(part):
    along_z = [[x * DEPTH + z for z in range(DEPTH)] for x in range(WIDTH)]
    along_x = [[x * DEPTH + z for x in range(WIDTH)] for z in range(DEPTH)]
    total = jnp.sum(spread(part, "group", 8), axis=0)
    column = spread(total, "curve", DEPTH, along_z)
    return spread(column, "curve", WIDTH, along_x)


def stage_pack(*args):
    outs = (
        ((192, 128), F32),
        ((192, 128), F32),
        ((64, 256), F32),
        ((88, 256), F32),
        ((8, 256), jnp.int32),
    )
    return call(pack_kernel, outs, (), "pack", 1 << 20, "hhhhhhhh", *args, limit=PACK_LIMIT)


def stage_prepare(*args):
    outs = (
        ((128, 2048), BF16),
        ((128, 64), BF16),
        ((128, 512), BF16),
        ((128, 512), BF16),
        ((32, 256), jnp.int32),
    )
    return call(prepare_kernel, outs, (), "prepare", 1 << 20, "vvvvvvvvvv", *args)


def stage_before(*args):
    outs = (((64, 384), F32), ((4, 128), F32))
    scratch = (
        ((64, 640), F32),
        ((64, 512), F32),
        ((88, 512), F32),
        ((88, 384), F32),
        ((64, 256), F32),
    )
    return call(before_kernel, outs, scratch, "before", 1 << 31, "v" * 9, *args)


def stage_finish(*args):
    outs = (((64, 256), F32),)
    return call(
        finish_kernel, outs, (((64, 384), F32),), "finish", 1 << 30, "v" * 10, *args
    )


def shards(
    right_side,
    start_field,
    block_level,
    neighbors,
    neighbor_kinds,
    owners_zero,
    owners_one,
    owners_two,
    owners_three,
    coarse_neighbors,
    coarse_kinds,
    coarse_level,
    stiffness,
    smoother,
    couplings,
    restriction,
):
    up, down, field, facts, parents = stage_pack(
        right_side,
        start_field,
        block_level[None, :],
        neighbors,
        neighbor_kinds,
        owners_zero,
        owners_one,
        owners_two,
    )
    left, right = both_ways(up, down)
    coupling_pair, smoother_pair, restriction_pair, back_pair, table = stage_prepare(
        couplings,
        stiffness,
        smoother,
        restriction,
        owners_one,
        owners_two,
        owners_three,
        coarse_neighbors,
        coarse_kinds,
        coarse_level[None, :],
    )
    iterate, part = stage_before(
        left,
        field,
        facts,
        right,
        parents,
        coupling_pair,
        smoother_pair,
        restriction_pair,
        table,
    )
    gathered = share_coarse(part)
    gathered = gathered.reshape(-1, gathered.shape[-1])
    (out,) = stage_finish(
        gathered,
        table,
        left,
        right,
        parents,
        coupling_pair,
        smoother_pair,
        back_pair,
        iterate,
        facts,
    )
    return out


def solution(mesh):
    fine = P(None, ("curve", "group"))
    return jax.shard_map(
        shards,
        mesh=mesh,
        in_specs=(
            fine,
            fine,
            P(("curve", "group")),
            fine,
            fine,
            fine,
            P(None, "curve"),
            P(None, "curve"),
            P(),
            P(),
            P(),
            P(),
            P(),
            P(),
            P(),
            P(),
        ),
        out_specs=fine,
        check_vma=False,
    )
```
